32 devices in a mesh: dp: 4 (over y, x), tensor: 8 (over z, core).
Axes of the slice: x: 2, y: 2, z: 4, core: 2. Of those that a mesh axis runs over, the one named last changes fastest.
Arguments:
- layer_input: bfloat16 [8192, 2048], P('dp'), may hold values from -6 to 6
- prefix_len: int32 [4], P('dp'), may hold values from 204 to 1024, as said below
- w_query: bfloat16 [2048, 2048], P(None, 'tensor'), may hold values from -0.1875 to 0.1875
- w_key: bfloat16 [2048, 2048], P(None, 'tensor'), may hold values from -0.1875 to 0.1875
- w_value: bfloat16 [2048, 2048], P(None, 'tensor'), may hold values from -0.125 to 0.125
- w_out: bfloat16 [2048, 2048], P('tensor'), may hold values from -0.5 to 0.5
- w_gate: bfloat16 [2048, 8192], P(None, 'tensor'), may hold values from -0.125 to 0.125
- w_up: bfloat16 [2048, 8192], P(None, 'tensor'), may hold values from -0.125 to 0.125
- w_down: bfloat16 [8192, 2048], P('tensor'), may hold values from -0.09375 to 0.09375
- cotangent: bfloat16 [8192, 2048], P(('dp', 'tensor')), may hold values from -6 to 6
Outputs:
- layer_output: float32 [8192, 2048], P(('dp', 'tensor'))
- input_grad: float32 [8192, 2048], P(('dp', 'tensor'))
- grad_query: float32 [2048, 2048], P('dp', 'tensor')
- grad_key: float32 [2048, 2048], P('dp', 'tensor')
- grad_value: float32 [2048, 2048], P('dp', 'tensor')
- grad_out: float32 [2048, 2048], P('tensor', 'dp')
- grad_gate: float32 [2048, 8192], P('dp', 'tensor')
- grad_up: float32 [2048, 8192], P('dp', 'tensor')
- grad_down: float32 [8192, 2048], P('tensor', 'dp')
The draws below stay inside these ranges and needn't reach their ends.
Inputs may be any that keep to these rules, and one draw needn't show every extreme that they name: `prefix_len`: each sequence has its own prefix length; some sequence's prefix is exactly half of 2048.
All inputs are finite; a program needn't handle non-finite values.
Results may differ from the reference program's by a relative error of at most 0.025.
Values may be sent and summed in bfloat16 or wider, within the bound.
No kernel may reach another device: no remote copies, remote signals or barrier semaphores. Data moves between devices by JAX's collectives and lax.ppermute only.
A program may use at most 320 MiB of HBM per device.

```python
import jax
import jax.numpy as jnp
from jax import lax

D = 2048
H = 16
HD = 128
FF = 8192
SEQ_LEN = 2048
SEQS = 4
TOKENS = 8192


def draw_prefix_len(key, part):
    first_key, second_key = jax.random.split(jax.random.fold_in(key, 11))
    lengths = jax.random.randint(first_key, (SEQS,), SEQ_LEN // 10, SEQ_LEN // 2 + 1, dtype=jnp.int32)
    chosen = jax.random.randint(second_key, (), 0, SEQS, dtype=jnp.int32)
    places = jnp.arange(SEQS, dtype=jnp.int32)
    return jnp.where(places == chosen, SEQ_LEN // 2, lengths).astype(jnp.int32)


def block_scale(stream_key, dims, cuts, least, top_value):
    loudness, own = 1.0, jax.random.fold_in(stream_key, 6)
    for axis_at, parts in cuts:
        heights = jnp.exp(jax.random.uniform(jax.random.fold_in(own, axis_at), (parts,), jnp.float32, least / len(cuts), top_value / len(cuts)))
        loudness = loudness * jnp.repeat(heights, dims[axis_at] // parts).reshape([-1 if axis == axis_at else 1 for axis in range(len(dims))])
    return loudness


def gaussian(rng, extent, spread, most, pieces=(), held_as=jnp.bfloat16):
    array = spread * jax.random.normal(rng, extent, jnp.float32)
    if pieces:
        array = array * block_scale(rng, extent, pieces, -0.22, 0.18)
    return jnp.clip(array, -most, most).astype(held_as)


def setup_inputs(seed: int = 0) -> dict:
    arg_keys = jax.random.split(jax.random.key(seed), 11)
    return {
        "layer_input": gaussian(arg_keys[0], (TOKENS, D), 1.0, 6.0, ((0, 4),)),
        "prefix_len": draw_prefix_len(jax.random.fold_in(arg_keys[10], 71), 0),
        "w_query": gaussian(arg_keys[2], (D, D), (D // 2) ** -0.5, 0.1875, ((1, 8),)),
        "w_key": gaussian(arg_keys[3], (D, D), (D // 2) ** -0.5, 0.1875, ((1, 8),)),
        "w_value": gaussian(arg_keys[4], (D, D), D ** -0.5, 0.125, ((1, 8),)),
        "w_out": gaussian(arg_keys[5], (D, D), (D // 16) ** -0.5, 0.5, ((0, 8),)),
        "w_gate": gaussian(arg_keys[6], (D, FF), D ** -0.5, 0.125, ((1, 8),)),
        "w_up": gaussian(arg_keys[7], (D, FF), D ** -0.5, 0.125, ((1, 8),)),
        "w_down": gaussian(arg_keys[8], (FF, D), (FF // 2) ** -0.5, 0.09375, ((0, 8),)),
        "cotangent": gaussian(arg_keys[9], (TOKENS, D), 1.0, 6.0, ((0, 32),)),
    }


@jax.custom_vjp
def low(v):
    return lax.optimization_barrier(v.astype(jnp.bfloat16)).astype(jnp.float32)

@jax.custom_vjp
def low_back(v):
    return v

def low_keep(v):
    return (low(v), None)

def low_pass(kept, grad):
    return (grad,)

def back_keep(v):
    return (v, None)

def back_low(kept, grad):
    return (low(grad),)
low.defvjp(low_keep, low_pass)
low_back.defvjp(back_keep, back_low)
epsilon = 1e-05
rope_base = 10000.0
masked_score = -1e+30

def matmul(left, right):
    return jnp.dot(left, right, precision=lax.Precision.HIGHEST)

def normalize(values):
    centered = values - lax.optimization_barrier(jnp.mean(values, -1, keepdims=True))
    return centered * lax.rsqrt(lax.optimization_barrier(jnp.mean(centered * centered, -1, keepdims=True)) + epsilon)

def rope_tables(seq_len, head_dim):
    inv_freq = rope_base ** (-(2.0 * jnp.arange(head_dim // 2, dtype=jnp.float32)) / head_dim)
    angles = jnp.arange(seq_len, dtype=jnp.float32)[:, None] * inv_freq[None, :]
    return (jnp.cos(angles), jnp.sin(angles))

def rotate(tensor, cos_table, sin_table):
    half_dim = tensor.shape[-1] // 2
    lead_part = tensor[..., :half_dim]
    tail_part = tensor[..., half_dim:]
    cos_part = cos_table[:, None, :]
    sin_part = sin_table[:, None, :]
    return jnp.concatenate([lead_part * cos_part - tail_part * sin_part, tail_part * cos_part + lead_part * sin_part], -1)

def head_attend(queries, key_rows, value_rows, prefix):
    block_rows = min(512, SEQ_LEN)
    score_scale = HD ** (-0.5)
    columns = jnp.arange(SEQ_LEN, dtype=jnp.int32)[None, :]

    def one_block(block_id):
        first_row = block_id * block_rows
        query_block = lax.dynamic_slice_in_dim(queries, first_row, block_rows, 0)
        scores = low_back(score_scale * matmul(query_block, key_rows.T))
        positions = first_row + jnp.arange(block_rows, dtype=jnp.int32)[:, None]
        allowed = (columns <= positions) | (columns < prefix)
        scores = jnp.where(allowed, scores, masked_score)
        probs = low(jax.nn.softmax(scores, axis=-1))
        return matmul(probs, value_rows)
    block_ids = jnp.arange(SEQ_LEN // block_rows, dtype=jnp.int32)
    return lax.map(jax.checkpoint(one_block), block_ids).reshape(SEQ_LEN, HD)

def layer_seq(inputs, prefix, w_query, w_key, w_value, w_out, w_gate, w_up, w_down):
    cos_table, sin_table = rope_tables(SEQ_LEN, HD)
    ln_one = low(normalize(inputs))
    query_lin = low_back(matmul(ln_one, w_query)).reshape(SEQ_LEN, H, HD)
    key_lin = low_back(matmul(ln_one, w_key)).reshape(SEQ_LEN, H, HD)
    queries = low(rotate(query_lin, cos_table, sin_table))
    key_rot = low(rotate(key_lin, cos_table, sin_table))
    values = low(low_back(matmul(ln_one, w_value))).reshape(SEQ_LEN, H, HD)

    def one_head(head_args):
        return head_attend(head_args[0], head_args[1], head_args[2], prefix)
    attended = lax.map(jax.checkpoint(one_head), (jnp.transpose(queries, (1, 0, 2)), jnp.transpose(key_rot, (1, 0, 2)), jnp.transpose(values, (1, 0, 2))))
    mixed = low(low_back(jnp.transpose(attended, (1, 0, 2)).reshape(SEQ_LEN, D)))
    residual = inputs + low_back(matmul(mixed, w_out))
    ln_two = low(normalize(residual))
    gate_lin = low_back(matmul(ln_two, w_gate))
    up_lin = low_back(matmul(ln_two, w_up))
    hidden = low(jax.nn.silu(gate_lin) * up_lin)
    return residual + matmul(hidden, w_down)

def reference(layer_input, prefix_len, w_query, w_key, w_value, w_out, w_gate, w_up, w_down, cotangent):

    def forward(inputs, query_w, key_w, value_w, out_w, gate_w, up_w, down_w):
        per_seq = inputs.reshape(SEQS, SEQ_LEN, D)

        def one_seq(seq_args):
            return layer_seq(seq_args[0], seq_args[1], query_w, key_w, value_w, out_w, gate_w, up_w, down_w)
        return lax.map(jax.checkpoint(one_seq), (per_seq, prefix_len)).reshape(SEQS * SEQ_LEN, D)
    floats = (layer_input.astype(jnp.float32), w_query.astype(jnp.float32), w_key.astype(jnp.float32), w_value.astype(jnp.float32), w_out.astype(jnp.float32), w_gate.astype(jnp.float32), w_up.astype(jnp.float32), w_down.astype(jnp.float32))
    layer_output, pullback = jax.vjp(forward, *floats)
    gradients = pullback(cotangent.astype(jnp.float32))
    return (layer_output, gradients[0], gradients[1], gradients[2], gradients[3], gradients[4], gradients[5], gradients[6], gradients[7])
```

```python
import math
from functools import partial

import jax
import jax.numpy as jnp
from jax import lax
from jax.experimental import pallas as pl
from jax.experimental.pallas import tpu as pltpu
from jax.sharding import PartitionSpec as P

HD = 128
EPS = 1e-05
ROPE_BASE = 10000.0
NEG = -1e30
LOG2E = math.log2(math.e)
Q_SCALE = LOG2E * HD**-0.5
F32 = jnp.float32
BF16 = jnp.bfloat16


def nt(a, b):
    return lax.dot_general(a, b, (((1,), (1,)), ((), ())), preferred_element_type=F32)


def nn(a, b):
    return lax.dot_general(a, b, (((1,), (0,)), ((), ())), preferred_element_type=F32)


def tn(a, b):
    return lax.dot_general(a, b, (((0,), (0,)), ((), ())), preferred_element_type=F32)


def normalize(values):
    centered = values - jnp.mean(values, -1, keepdims=True)
    inv_std = lax.rsqrt(jnp.mean(centered * centered, -1, keepdims=True) + EPS)
    return centered * inv_std, inv_std


def norm_back(normed, inv_std, upstream):
    first_mean = jnp.mean(upstream, -1, keepdims=True)
    second_mean = jnp.mean(upstream * normed, -1, keepdims=True)
    return inv_std * (upstream - first_mean - normed * second_mean)


def rope_tables(seq_len, coarse=64):
    inv_freq = ROPE_BASE ** (-(2.0 * jnp.arange(HD // 2, dtype=F32)) / HD)
    fine = jnp.arange(coarse, dtype=F32)[:, None] * inv_freq[None, :]
    steps = (coarse * jnp.arange(seq_len // coarse, dtype=F32))[:, None] * inv_freq[None, :]
    both = lax.optimization_barrier((jnp.cos(fine), jnp.sin(fine), jnp.cos(steps), jnp.sin(steps)))
    cb, sb, ca, sa = both[0][None], both[1][None], both[2][:, None], both[3][:, None]
    cos = (ca * cb - sa * sb).reshape(seq_len, HD // 2)
    sin = (sa * cb + ca * sb).reshape(seq_len, HD // 2)
    return jnp.concatenate([cos, cos], -1), jnp.concatenate([-sin, sin], -1)


def qkv_kernel(x_ref, wq_ref, wk_ref, wv_ref, cos_ref, sin_ref, ln_ref, q_ref, k_ref, kt_ref, v_ref, vt_ref):
    normed, _ = normalize(x_ref[...].astype(F32))
    ln = normed.astype(BF16)
    ln_ref[...] = ln
    cos, sin = cos_ref[...], sin_ref[...]
    q, k, v = nn(ln, wq_ref[...]), nn(ln, wk_ref[...]), nn(ln, wv_ref[...]).astype(BF16)
    for h in range(q.shape[1] // HD):
        at = slice(h * HD, (h + 1) * HD)
        qh, kh = q[:, at], k[:, at]
        qr = (qh * cos + pltpu.roll(qh, HD // 2, 1) * sin) * Q_SCALE
        kr = (kh * cos + pltpu.roll(kh, HD // 2, 1) * sin).astype(BF16)
        q_ref[:, at] = qr.astype(BF16)
        k_ref[:, at] = kr
        kt_ref[at, :] = kr.T
        vt_ref[at, :] = v[:, at].T
    v_ref[...] = v


def qkv(x, w_query, w_key, w_value, cos, sin, block=256):
    rows, width = x.shape
    dim = w_query.shape[1]
    by_row = lambda n: pl.BlockSpec((block, n), lambda i: (i, 0))
    whole = pl.BlockSpec((width, dim), lambda i: (0, 0))
    flipped = pl.BlockSpec((dim, block), lambda i: (0, i))
    shape = lambda *dims: jax.ShapeDtypeStruct(dims, BF16)
    return pl.pallas_call(
        qkv_kernel,
        grid=(rows // block,),
        in_specs=[by_row(width), whole, whole, whole, by_row(HD), by_row(HD)],
        out_specs=[by_row(width), by_row(dim), by_row(dim), flipped, by_row(dim), flipped],
        out_shape=[
            shape(rows, width),
            shape(rows, dim),
            shape(rows, dim),
            shape(dim, rows),
            shape(rows, dim),
            shape(dim, rows),
        ],
        compiler_params=pltpu.CompilerParams(vmem_limit_bytes=40 << 20),
        cost_estimate=pl.CostEstimate(
            flops=6 * rows * width * dim, bytes_accessed=4 * rows * width + 6 * width * dim + 10 * rows * dim, transcendentals=0
        ),
        name="qkv",
    )(x, w_query, w_key, w_value, cos, sin)


def allowed_mask(key0, q0, shape, prefix):
    cols = key0 + lax.broadcasted_iota(jnp.int32, shape, 0)
    rows = q0 + lax.broadcasted_iota(jnp.int32, shape, 1)
    return (cols <= rows) | (cols < prefix)


def key_blocks(q0, bq, bk, prefix):
    full = jnp.maximum((q0 + 1) // bk, prefix // bk)
    total = jnp.maximum((q0 + bq + bk - 1) // bk, (prefix + bk - 1) // bk)
    return full, total


def fwd_kernel(prefix_ref, q_ref, k_ref, vt_ref, o_ref, lse_ref, m_s, l_s, acc_s, *, row0, bq, bk):
    prefix = prefix_ref[0]
    q0 = row0 + pl.program_id(1) * bq
    q = q_ref[...]
    m_s[...] = jnp.full(m_s.shape, NEG, F32)
    l_s[...] = jnp.zeros(l_s.shape, F32)
    acc_s[...] = jnp.zeros(acc_s.shape, F32)

    def step(j, masked):
        k0 = pl.multiple_of(j * bk, bk)
        s = nt(k_ref[pl.ds(k0, bk), :], q)
        if masked:
            s = jnp.where(allowed_mask(k0, q0, s.shape, prefix), s, NEG)
        m_old = m_s[...]
        m_new = jnp.maximum(m_old, jnp.max(s, 0, keepdims=True))
        p = jnp.exp2(s - m_new)
        a = jnp.exp2(m_old - m_new)
        l_s[...] = l_s[...] * a + jnp.sum(p, 0, keepdims=True)
        acc_s[...] = acc_s[...] * a + nn(vt_ref[:, pl.ds(k0, bk)], p.astype(BF16))
        m_s[...] = m_new

    full, total = key_blocks(q0, bq, bk, prefix)
    lax.fori_loop(0, full, lambda j, c: (step(j, False), c)[1], 0)
    lax.fori_loop(full, total, lambda j, c: (step(j, True), c)[1], 0)
    l = l_s[...]
    o_ref[...] = (acc_s[...] / l).T.astype(BF16)
    lse_ref[...] = (m_s[...] + jnp.log2(l))[None]


def attn_fwd(q, k, vt, prefix, row0, rows, bq=512, bk=512):
    seq, dim = k.shape
    heads = dim // HD
    bq, bk = min(bq, rows), min(bk, rows)
    first = row0 // bq
    return pl.pallas_call(
        partial(fwd_kernel, row0=row0, bq=bq, bk=bk),
        grid_spec=pltpu.PrefetchScalarGridSpec(
            num_scalar_prefetch=1,
            grid=(heads, rows // bq),
            in_specs=[
                pl.BlockSpec((bq, HD), lambda h, i, p: (i + first, h)),
                pl.BlockSpec((seq, HD), lambda h, i, p: (0, h)),
                pl.BlockSpec((HD, seq), lambda h, i, p: (h, 0)),
            ],
            out_specs=[
                pl.BlockSpec((bq, HD), lambda h, i, p: (i, h)),
                pl.BlockSpec((1, 1, bq), lambda h, i, p: (h, 0, i)),
            ],
            scratch_shapes=[
                pltpu.VMEM((1, bq), F32),
                pltpu.VMEM((1, bq), F32),
                pltpu.VMEM((HD, bq), F32),
            ],
        ),
        out_shape=[
            jax.ShapeDtypeStruct((rows, dim), BF16),
            jax.ShapeDtypeStruct((heads, 1, rows), F32),
        ],
        compiler_params=pltpu.CompilerParams(vmem_limit_bytes=32 << 20),
        cost_estimate=pl.CostEstimate(
            flops=12 * rows * seq * dim, bytes_accessed=4 * seq * dim + 4 * rows * dim, transcendentals=rows * seq * heads
        ),
        name="attn_fwd",
    )(prefix, q, k, vt)


def unrope(t, cos, sin):
    return t * cos - pltpu.roll(t, HD // 2, 1) * sin


def bwd_kernel(prefix_ref, q_ref, k_ref, kt_ref, v_ref, o_ref, do_ref, lse_ref, cq_ref, sq_ref, ck_ref, sk_ref, *rest, row0, bq, bk, keys, has_in, lo):
    rest = list(rest)
    if has_in:
        dk_in, dv_in = rest[:2]
        rest = rest[2:]
    dq_ref, dk_ref, dv_ref = rest[:3]
    rest = rest[3:]
    if lo:
        dk_part, dv_part = rest[:2]
        rest = rest[2:]
    dk_s, dv_s, dq_s = rest
    qi = pl.program_id(1)
    prefix = prefix_ref[0]
    q0 = row0 + qi * bq

    @pl.when(qi == 0)
    def _():
        if has_in:
            dk_s[...] = dk_in[...]
            dv_s[...] = dv_in[...]
        else:
            dk_s[...] = jnp.zeros(dk_s.shape, F32)
            dv_s[...] = jnp.zeros(dv_s.shape, F32)

    q, do = q_ref[...], do_ref[...]
    lse = lse_ref[0]
    delta = jnp.sum((do.astype(F32) * o_ref[...].astype(F32)).T, 0, keepdims=True)
    dq_s[...] = jnp.zeros(dq_s.shape, F32)

    def step(j, masked):
        k0 = pl.multiple_of(j * bk, bk)
        at = pl.ds(k0, bk)
        s = nt(k_ref[at, :], q)
        p = jnp.exp2(s - lse)
        if masked:
            p = jnp.where(allowed_mask(k0, q0, s.shape, prefix), p, 0.0)
        dp = nt(v_ref[at, :], do)
        ds = (p * (dp - delta)).astype(BF16)
        dv_s[at, :] += nn(p.astype(BF16), do)
        dk_s[at, :] += nn(ds, q)
        dq_s[...] += nn(kt_ref[:, at], ds)

    full, total = key_blocks(q0, bq, bk, prefix)
    lax.fori_loop(0, full, lambda j, c: (step(j, False), c)[1], 0)
    lax.fori_loop(full, total, lambda j, c: (step(j, True), c)[1], 0)
    dq_ref[...] = unrope((dq_s[...] * HD**-0.5).T, cq_ref[...], sq_ref[...]).astype(BF16)

    @pl.when(qi == pl.num_programs(1) - 1)
    def _():
        dk_ref[...] = unrope(dk_s[lo:keys, :] * (1.0 / LOG2E), ck_ref[...], sk_ref[...]).astype(BF16)
        dv_ref[...] = dv_s[lo:keys, :].astype(BF16)
        if lo:
            dk_part[...] = dk_s[:lo, :]
            dv_part[...] = dv_s[:lo, :]


def attn_bwd(q, k, kt, v, o, do, lse, cos, sin, prefix, row0, rows, lo, part=None, bq=512, bk=512):
    dim = k.shape[1]
    heads = dim // HD
    keys = row0 + rows
    own = keys - lo
    bq, bk = min(bq, rows), min(bk, rows)
    first = row0 // bq
    has_in = part is not None
    full = lambda n: pl.BlockSpec((n, HD), lambda h, i, p: (0, h))
    table_q = pl.BlockSpec((bq, HD), lambda h, i, p: (i + first, 0))
    table_k = pl.BlockSpec((own, HD), lambda h, i, p: (lo // own, 0))
    by_q = pl.BlockSpec((bq, HD), lambda h, i, p: (i, h))
    in_specs = [
        pl.BlockSpec((bq, HD), lambda h, i, p: (i + first, h)),
        full(keys),
        pl.BlockSpec((HD, keys), lambda h, i, p: (h, 0)),
        full(keys),
        by_q,
        by_q,
        pl.BlockSpec((1, 1, bq), lambda h, i, p: (h, 0, i)),
        table_q,
        table_q,
        table_k,
        table_k,
    ]
    args = [q, k, kt, v, o, do, lse, cos, sin, cos, sin]
    if has_in:
        in_specs += [full(keys), full(keys)]
        args += list(part)
    out_specs = [by_q, full(own), full(own)]
    out_shape = [jax.ShapeDtypeStruct((rows, dim), BF16)] + [jax.ShapeDtypeStruct((own, dim), BF16)] * 2
    if lo:
        out_specs += [full(lo), full(lo)]
        out_shape += [jax.ShapeDtypeStruct((lo, dim), F32)] * 2
    return pl.pallas_call(
        partial(bwd_kernel, row0=row0, bq=bq, bk=bk, keys=keys, has_in=has_in, lo=lo),
        grid_spec=pltpu.PrefetchScalarGridSpec(
            num_scalar_prefetch=1,
            grid=(heads, rows // bq),
            in_specs=in_specs,
            out_specs=out_specs,
            scratch_shapes=[
                pltpu.VMEM((keys, HD), F32),
                pltpu.VMEM((keys, HD), F32),
                pltpu.VMEM((HD, bq), F32),
            ],
        ),
        out_shape=out_shape,
        compiler_params=pltpu.CompilerParams(vmem_limit_bytes=48 << 20),
        cost_estimate=pl.CostEstimate(
            flops=24 * rows * keys * dim, bytes_accessed=8 * keys * dim + 8 * rows * dim, transcendentals=rows * keys * heads
        ),
        name="attn_bwd",
    )(prefix, *args)


def resident(a):
    return pl.BlockSpec(a.shape, lambda *_: (0,) * a.ndim, pipeline_mode=pl.Buffered(1))


def call(kernel, grid, in_specs, out_specs, out_shape, name, flops, traffic, scratch=(), prefetch=1, vmem=56, exps=0):
    return pl.pallas_call(
        kernel,
        grid_spec=pltpu.PrefetchScalarGridSpec(
            num_scalar_prefetch=prefetch,
            grid=grid,
            in_specs=in_specs,
            out_specs=out_specs,
            scratch_shapes=list(scratch),
        ),
        out_shape=out_shape,
        compiler_params=pltpu.CompilerParams(vmem_limit_bytes=vmem << 20),
        cost_estimate=pl.CostEstimate(flops=flops, bytes_accessed=traffic, transcendentals=exps),
        name=name,
    )


def bf16(*dims):
    return jax.ShapeDtypeStruct(dims, BF16)


def split_matmul_kernel(at_ref, *refs, terms):
    share = refs[-1].shape[0]
    xs, ws, (keep_ref, send_ref, both) = refs[:terms], refs[terms : 2 * terms], refs[2 * terms :]
    total = nt(xs[0][...], ws[0][...]) if terms > 1 else nn(xs[0][...], ws[0][...])
    for x, w in zip(xs[1:], ws[1:]):
        total = total + nt(x[...], w[...])
    both[...] = total.astype(BF16)
    share = keep_ref.shape[0]
    core = at_ref[0]
    keep_ref[...] = both[pl.ds(pl.multiple_of(core * share, share), share), :]
    send_ref[...] = both[pl.ds(pl.multiple_of((1 - core) * share, share), share), :]


def split_matmul(at, xs, ws, share):
    rows = xs[0].shape[0]
    depth = sum(x.shape[1] for x in xs)
    width = ws[0].shape[1] if len(xs) == 1 else ws[0].shape[0]
    block = 2 * share
    return call(
        partial(split_matmul_kernel, terms=len(xs)),
        (rows // block,),
        [pl.BlockSpec((block, x.shape[1]), lambda i, a: (i, 0)) for x in xs] + [resident(w) for w in ws],
        [pl.BlockSpec((share, width), lambda i, a: (i, 0))] * 2,
        [bf16(rows // 2, width)] * 2,
        "split_matmul",
        2 * rows * depth * width,
        2 * rows * (depth + width) + 2 * depth * width,
        scratch=[pltpu.VMEM((block, width), BF16)],
        vmem=40,
    )(at, *xs, *ws)


def doubling_order(chips):
    order, hop = [0], chips // 2
    while hop:
        order = order + [o ^ hop for o in order]
        hop //= 2
    return order


def assemble_kernel(at_ref, *refs, order):
    pieces, out = refs[:-1], refs[-1]
    share = out.shape[0]
    want = lax.bitwise_xor(at_ref[1], pl.program_id(0))
    j = 0
    for piece in pieces:
        for s in range(piece.shape[0] // share):

            @pl.when(want == order[j])
            def _():
                out[...] = piece[s * share : (s + 1) * share, :]

            j += 1


def assemble(at, pieces):
    share, width = pieces[0].shape
    chips = sum(p.shape[0] for p in pieces) // share
    return call(
        partial(assemble_kernel, order=doubling_order(chips)),
        (chips,),
        [resident(p) for p in pieces],
        pl.BlockSpec((share, width), lambda i, a: (i, 0)),
        bf16(chips * share, width),
        "assemble",
        0,
        4 * chips * share * width,
        vmem=40,
    )(at, *pieces)


def ff_kernel(
    at_ref, mixed_ref, x_ref, cot_ref, wm_ref, wo_ref, wg_ref, wu_ref, wd_ref,
    res_ref, ln_ref, hid_ref, gg_ref, gu_ref, keep_ref, send_ref, back,
):
    core, chip = at_ref[0], at_ref[1]
    share, dim = res_ref.shape[0], mixed_ref.shape[2]
    chips = mixed_ref.shape[0] // 2
    residual = x_ref[...].astype(F32)
    for z in range(chips):
        rows = pl.ds(pl.multiple_of(at_ref[2 + z] * dim, dim), dim)
        residual = residual + nn(mixed_ref[2 * z + core], wm_ref[rows, :])
        residual = residual + nn(mixed_ref[2 * z + 1 - core], wo_ref[rows, :])

    @pl.when(pl.program_id(0) == chip)
    def _():
        res_ref[...] = jnp.where(core == 0, residual[:share, :], residual[share:, :])

    normed, _ = normalize(residual)
    ln = normed.astype(BF16)
    ln_ref[...] = ln
    gate = nn(ln, wg_ref[...])
    up = nn(ln, wu_ref[...])
    grad = nt(cot_ref[...], wd_ref[...])
    sig = 1.0 / (1.0 + jnp.exp(-gate))
    act = gate * sig
    hid_ref[...] = (act * up).astype(BF16)
    gg = (grad * up * sig * (1.0 + gate * (1.0 - sig))).astype(BF16)
    gu = (grad * act).astype(BF16)
    gg_ref[...] = gg
    gu_ref[...] = gu
    back[...] = (nt(gg, wg_ref[...]) + nt(gu, wu_ref[...])).astype(BF16)
    keep_ref[...] = back[pl.ds(pl.multiple_of(core * share, share), share), :]
    send_ref[...] = back[pl.ds(pl.multiple_of((1 - core) * share, share), share), :]


def feed_forward(at, mixed, x, cot, row0, w_mine, w_other, w_gate, w_up, w_down, share):
    n, rows, dim = mixed.shape
    width = x.shape[1]
    hid = w_gate.shape[1]
    block = 2 * share
    first = row0 // block
    by_row = lambda n, f=0: pl.BlockSpec((block, n), lambda i, a: (i + f, 0))
    by_share = pl.BlockSpec((share, width), lambda i, a: (i, 0))
    return call(
        ff_kernel,
        (rows // block,),
        [
            pl.BlockSpec((n, block, dim), lambda i, a: (0, i, 0)),
            by_row(width, first),
            by_row(width, first),
            resident(w_mine),
            resident(w_other),
            resident(w_gate),
            resident(w_up),
            resident(w_down),
        ],
        [pl.BlockSpec((share, width), lambda i, a: (0, 0)), by_row(width), by_row(hid), by_row(hid), by_row(hid)]
        + [by_share] * 2,
        [jax.ShapeDtypeStruct((share, width), F32), bf16(rows, width)]
        + [bf16(rows, hid)] * 3
        + [bf16(rows // 2, width)] * 2,
        "feed_forward",
        10 * rows * width * hid + 2 * rows * width * width,
        6 * width * hid + 2 * width * width + 10 * rows * width + 6 * rows * hid,
        scratch=[pltpu.VMEM((block, width), BF16)],
        exps=rows * hid,
    )(at, mixed, x, cot, w_mine, w_other, w_gate, w_up, w_down)


def ffn_out_kernel(at_ref, lo_ref, hi_ref, rlo_ref, rhi_ref, w_ref, keep_ref, send_ref, out, *, steps):
    share = rlo_ref.shape[0]
    core, chip = at_ref[0], at_ref[1]
    step = pl.program_id(0)
    for base, hid_ref, res_ref in ((0, lo_ref, rlo_ref), (steps // 2, hi_ref, rhi_ref)):
        inside = step - base

        @pl.when(jnp.logical_and(inside >= 0, inside < steps // 2))
        def _():
            out[...] = nn(hid_ref[...], w_ref[...])

            @pl.when(inside == chip)
            def _():
                mine = pl.ds(pl.multiple_of(core * share, share), share)
                out[mine, :] = out[mine, :] + res_ref[...]

    ours = lax.rem(step, 2) == core

    @pl.when(ours)
    def _():
        keep_ref[...] = out[...].astype(BF16)

    @pl.when(jnp.logical_not(ours))
    def _():
        send_ref[...] = out[...].astype(BF16)


def ffn_out(at, hid_lo, hid_hi, res_lo, res_hi, w_down):
    half, hid = hid_lo.shape
    share, width = res_lo.shape
    block = 2 * share
    steps = 2 * half // block
    per = steps // 2
    by_pair = pl.BlockSpec((block, width), lambda i, a: (i // 2, 0))
    return call(
        partial(ffn_out_kernel, steps=steps),
        (steps,),
        [
            pl.BlockSpec((block, hid), lambda i, a: (jnp.minimum(i, per - 1), 0)),
            pl.BlockSpec((block, hid), lambda i, a: (jnp.maximum(i - per, 0), 0)),
            resident(res_lo),
            resident(res_hi),
            resident(w_down),
        ],
        [by_pair, by_pair],
        [bf16(half, width)] * 2,
        "ffn_out",
        4 * half * hid * width,
        4 * half * (hid + width) + 2 * hid * width,
        scratch=[pltpu.VMEM((block, width), F32)],
        vmem=40,
    )(at, hid_lo, hid_hi, res_lo, res_hi, w_down)


def columns_kernel(dp_ref, *refs):
    pieces, out = refs[:-1], refs[-1]
    for s, piece in enumerate(pieces):

        @pl.when(lax.bitwise_xor(dp_ref[0], pl.program_id(0)) == s)
        def _():
            out[...] = piece[...]


def columns(dp, pieces):
    rows, part = pieces[0].shape
    n = len(pieces)
    return call(
        columns_kernel,
        (n,),
        [resident(p) for p in pieces],
        pl.BlockSpec((rows, part), lambda i, a: (0, i)),
        bf16(rows, n * part),
        "columns",
        0,
        4 * n * rows * part,
        vmem=40,
    )(dp, *pieces)


def grad_mixed_kernel(at_ref, gm_ref, go_ref, w_ref, rows_ref, out_ref):
    share = gm_ref.shape[0]
    core = at_ref[0]
    rows_ref[pl.ds(pl.multiple_of(core * share, share), share), :] = gm_ref[...]
    rows_ref[pl.ds(pl.multiple_of((1 - core) * share, share), share), :] = go_ref[...]
    out_ref[...] = nt(rows_ref[...], w_ref[...]).astype(BF16)


def grad_mixed(at, mine, other, w_out, share):
    half, width = mine.shape
    dim = w_out.shape[0]
    block = 2 * share
    by_share = pl.BlockSpec((share, width), lambda i, a: (i, 0))
    return call(
        grad_mixed_kernel,
        (half // share,),
        [by_share, by_share, resident(w_out)],
        [pl.BlockSpec((block, width), lambda i, a: (i, 0)), pl.BlockSpec((block, dim), lambda i, a: (i, 0))],
        [bf16(2 * half, width), bf16(2 * half, dim)],
        "grad_mixed",
        4 * half * width * dim,
        8 * half * width + 2 * width * dim,
        vmem=40,
    )(at, mine, other, w_out)


def wgrad_kernel(at_ref, *refs, groups):
    out = refs[-1]
    used, col = 0, 0
    for pieces, count in groups:
        a = refs[used : used + pieces]
        used += pieces
        for _ in range(count):
            b = refs[used : used + pieces]
            used += pieces
            total = tn(a[0][...], b[0][...])
            for s in range(1, pieces):
                total = total + tn(a[s][...], b[s][...])
            out[:, col : col + total.shape[1]] = total.astype(BF16)
            col += total.shape[1]


def wgrad(at, groups, block=512):
    in_specs, args, kinds, cols, flops = [], [], [], 0, 0
    for a, bs in groups:
        for piece in a:
            array, rows, at_row = piece if isinstance(piece, tuple) else (piece, piece.shape[0], 0)
            wide = array.shape[1]
            size = min(block, wide)
            in_specs.append(pl.BlockSpec((rows, size), lambda i, g, r=at_row: (r, i)))
            args.append(array)
        for b in bs:
            for piece in b:
                array, rows, at_row = piece if isinstance(piece, tuple) else (piece, piece.shape[0], 0)
                in_specs.append(
                    pl.BlockSpec(
                        (rows, array.shape[1]), lambda i, g, r=at_row: (r, 0), pipeline_mode=pl.Buffered(1)
                    )
                )
                args.append(array)
                flops += 2 * wide * rows * array.shape[1]
            cols += array.shape[1]
        kinds.append((len(a), len(bs)))
    return call(
        partial(wgrad_kernel, groups=kinds),
        (wide // size,),
        in_specs,
        pl.BlockSpec((size, cols), lambda i, g: (i, 0)),
        bf16(wide, cols),
        "wgrad",
        flops,
        4 * wide * cols + sum(2 * x.size for x in args),
    )(at, *args)


def add(a, b):
    return (a.astype(F32) + b.astype(F32)).astype(BF16)


def local(layer_input, prefix_len, w_query, w_key, w_value, w_out, w_gate, w_up, w_down, cotangent):
    seq, width = layer_input.shape
    n = lax.axis_size("tensor")
    chips = n // 2
    stages = chips.bit_length() - 1
    place = lax.axis_index("tensor")
    chip, core = place // 2, lax.rem(place, 2)
    half = seq // 2
    share = half // n
    block = seq // n
    found = [doubling_order(chips).index(z) for z in range(chips)]
    at = jnp.concatenate([jnp.stack([core, chip]), jnp.array(found)[lax.bitwise_xor(chip, jnp.arange(chips))]])
    at = at.astype(jnp.int32)
    latest = [None]

    def done(value):
        latest[0] = value
        return value

    def later(value):
        if latest[0] is None:
            return value
        return lax.optimization_barrier((value, latest[0]))[0]

    def my_rows(matrix, first):
        return lax.dynamic_slice_in_dim(matrix, first + place * share, share, 0)

    def start(x, pairs):
        return lax.ppermute(later(x), "tensor", pairs)

    swap_cores = [(t, t ^ 1) for t in range(n)]

    def chips_apart(hop):
        return [(t, t ^ (2 * hop)) for t in range(n)]

    class Gather:
        def __init__(self, own):
            self.pieces = [own]
            self.hop = chips // 2
            self.coming = start(own, chips_apart(self.hop))

        def step(self):
            self.pieces.append(done(later(self.coming)))
            self.hop //= 2
            if self.hop:
                self.coming = start(done(jnp.concatenate(self.pieces, 0)), chips_apart(self.hop))
            else:
                self.mine = done(assemble(later(at), self.pieces))
                self.other = start(self.mine, swap_cores)

    class Scatter:
        def __init__(self, keep, sent):
            self.held = keep.reshape(chips, -1, width)
            self.coming = start(sent, swap_cores).reshape(self.held.shape)
            self.hop = 1

        def step(self):
            total = add(self.held, later(self.coming))
            if self.hop == chips:
                return done(total[0])
            bit = lax.rem(chip // self.hop, 2)
            pairs = total.reshape(total.shape[0] // 2, 2, -1, width)
            self.held = lax.dynamic_index_in_dim(pairs, bit, 1, False)
            sent = done(lax.dynamic_index_in_dim(pairs, 1 - bit, 1, False))
            self.coming = lax.ppermute(sent, "tensor", chips_apart(self.hop))
            self.hop *= 2

    starts = {"hi": half, "lo": 0}
    hi, lo = {}, {}
    halves = {"hi": hi, "lo": lo}

    def attention(name):
        c = halves[name]
        c["mixed"], c["lse"] = attn_fwd(later(q), k, vt, prefix_len, starts[name], half)
        c["all_mixed"] = lax.all_gather(done(c["mixed"]), "tensor")

    def both_ways(name):
        c = halves[name]
        c["residual"], c["ln"], c["hidden"], c["g_gate"], c["g_up"], c["keep"], c["send"] = feed_forward(
            at, later(c["all_mixed"]), layer_input, cot, starts[name], *w_full, w_gate, w_up, w_down, share
        )
        done(c["keep"])

    def residual_grad(name):
        c = halves[name]
        total = c["g_norm"].step().astype(F32)
        back = norm_back(*normalize(c["residual"]), total)
        c["g_res_rows"] = my_rows(cot, starts[name]).astype(F32) + back
        c["g_rows"] = Gather(done(c["g_res_rows"].astype(BF16)))

    part = None

    def attention_back(name):
        nonlocal part
        c = halves[name]
        first = starts[name]
        other = later(c["g_rows"].other)
        c["g_res"], g_mixed = grad_mixed(at, c["g_rows"].mine, other, w_out, share)
        done(g_mixed)
        grads = attn_bwd(q, k, kt, v, c["mixed"], g_mixed, c["lse"], cos, sin, prefix_len, first, half, first, part)
        c["dq"], c["dk"], c["dv"] = grads[:3]
        part = grads[3:]
        done(c["dq"])
        c["keep"], c["send"] = split_matmul(later(at), [c["dq"], c["dk"], c["dv"]], [w_query, w_key, w_value], share)
        done(c["keep"])

    def to_dp(grad, dim):
        return lax.psum_scatter(grad, "dp", scatter_dimension=dim, tiled=True)

    def input_rows(name):
        c = halves[name]
        first = starts[name]
        normed, inv = normalize(my_rows(layer_input, first).astype(F32))
        total = c["g_one"].step().astype(F32)
        rows = done((c["g_res_rows"] + norm_back(normed, inv, total)).astype(BF16))
        base = first // block
        c["moved"] = [
            lax.ppermute(rows, "tensor", [(t, base + t // 2) for t in range(odd, n, 2)]) for odd in range(2)
        ]

    def more(transfer):
        for _ in range(stages - 1):
            transfer.step()

    n_dp = lax.axis_size("dp")
    dp_place = lax.axis_index("dp")
    piece = lax.dynamic_slice_in_dim(w_out, dp_place * (width // n_dp), width // n_dp, 1)
    hop = chips // 2
    coming = start(piece, chips_apart(hop))
    cot = lax.all_gather(cotangent, "tensor", axis=0, tiled=True)
    cos, sin = rope_tables(seq)
    done(cos)
    piece = jnp.concatenate([piece, later(coming)], 0)
    first = True
    while hop > 1:
        hop //= 2
        coming = start(done(piece), chips_apart(hop))
        if first:
            ln_one, q, k, kt, v, vt = qkv(layer_input, w_query, w_key, w_value, later(cos), sin)
            done(q)
            attention("hi")
            first = False
        piece = jnp.concatenate([piece, later(coming)], 0)
    pieces = [done(piece)] + [lax.ppermute(piece, "dp", [(d, d ^ s) for d in range(n_dp)]) for s in range(1, n_dp)]
    attention("lo")
    w_mine = done(columns(dp_place.astype(jnp.int32)[None], [later(p) for p in pieces]))
    w_full = [w_mine, lax.ppermute(w_mine, "tensor", swap_cores)]
    cot = done(later(cot))
    both_ways("hi")
    hi["g_norm"] = Scatter(hi["keep"], hi["send"])
    hi["g_norm"].step()
    both_ways("lo")
    more(hi["g_norm"])
    lo["g_norm"] = Scatter(lo["keep"], lo["send"])
    keep, sent = ffn_out(at, later(lo["hidden"]), hi["hidden"], lo["residual"], hi["residual"], w_down)
    done(keep)
    lo["g_norm"].step()
    residual_grad("hi")
    grad_gate_up = done(
        wgrad(at, [([hi["ln"], later(lo["ln"])], [[hi["g_gate"], lo["g_gate"]], [hi["g_up"], lo["g_up"]]])])
    )
    more(lo["g_norm"])
    more(hi["g_rows"])
    grad_gate_up = to_dp(grad_gate_up, 0)
    residual_grad("lo")
    ffn = Scatter(keep, sent)
    grad_down = done(wgrad(at, [([hi["hidden"], later(lo["hidden"])], [[(cot, half, 1), (cot, half, 0)]])]))
    hi["g_rows"].step()
    grad_down = to_dp(grad_down, 1)
    attention_back("hi")
    more(lo["g_rows"])
    ffn.step()
    hi["g_one"] = Scatter(hi["keep"], hi["send"])
    hi["g_one"].step()
    lo["g_rows"].step()
    attention_back("lo")
    more(hi["g_one"])
    more(ffn)
    lo["g_one"] = Scatter(lo["keep"], lo["send"])
    lo["g_one"].step()
    rows = ln_one.shape[0] // 2
    grads = done(
        wgrad(
            at,
            [
                ([(later(ln_one), rows, 0), (ln_one, rows, 1)], [[lo[key], hi[key]] for key in ("dq", "dk", "dv")]),
                ([lo["g_res"], hi["g_res"]], [[lo["mixed"], hi["mixed"]]]),
            ],
        )
    )
    grads = to_dp(grads, 0)
    more(lo["g_one"])
    input_rows("hi")
    layer_output = ffn.step().astype(F32)
    input_rows("lo")
    input_grad = sum(jnp.concatenate(c["moved"], 0).astype(F32) for c in halves.values())
    hid, dim = w_gate.shape[1], w_query.shape[1]
    grads, grad_gate_up = grads.astype(F32), grad_gate_up.astype(F32)
    return (
        layer_output,
        input_grad,
        grads[:, :dim],
        grads[:, dim : 2 * dim],
        grads[:, 2 * dim : 3 * dim],
        grads[:, 3 * dim :].T,
        grad_gate_up[:, :hid],
        grad_gate_up[:, hid:],
        grad_down.astype(F32),
    )


def solution(mesh):
    in_specs = (
        P("dp", None),
        P("dp"),
        P(None, "tensor"),
        P(None, "tensor"),
        P(None, "tensor"),
        P("tensor", None),
        P(None, "tensor"),
        P(None, "tensor"),
        P("tensor", None),
        P(("dp", "tensor"), None),
    )
    out_specs = (
        P(("dp", "tensor"), None),
        P(("dp", "tensor"), None),
        P("dp", "tensor"),
        P("dp", "tensor"),
        P("dp", "tensor"),
        P("tensor", "dp"),
        P("dp", "tensor"),
        P("dp", "tensor"),
        P("tensor", "dp"),
    )
    return jax.shard_map(local, mesh=mesh, in_specs=in_specs, out_specs=out_specs, check_vma=False)
```

```python
import math
from functools import partial

import jax
import jax.numpy as jnp
from jax import lax
from jax.experimental import pallas as pl
from jax.experimental.pallas import tpu as pltpu
from jax.sharding import PartitionSpec as P

HD = 128
EPS = 1e-05
ROPE_BASE = 10000.0
NEG = -1e30
LOG2E = math.log2(math.e)
Q_SCALE = LOG2E * HD**-0.5
F32 = jnp.float32
BF16 = jnp.bfloat16


def nt(a, b):
    return lax.dot_general(a, b, (((1,), (1,)), ((), ())), preferred_element_type=F32)


def nn(a, b):
    return lax.dot_general(a, b, (((1,), (0,)), ((), ())), preferred_element_type=F32)


def tn(a, b):
    return lax.dot_general(a, b, (((0,), (0,)), ((), ())), preferred_element_type=F32)


def normalize(values):
    centered = values - jnp.mean(values, -1, keepdims=True)
    inv_std = lax.rsqrt(jnp.mean(centered * centered, -1, keepdims=True) + EPS)
    return centered * inv_std, inv_std


def norm_back(normed, inv_std, upstream):
    first_mean = jnp.mean(upstream, -1, keepdims=True)
    second_mean = jnp.mean(upstream * normed, -1, keepdims=True)
    return inv_std * (upstream - first_mean - normed * second_mean)


def rope_tables(seq_len, coarse=64):
    inv_freq = ROPE_BASE ** (-(2.0 * jnp.arange(HD // 2, dtype=F32)) / HD)
    fine = jnp.arange(coarse, dtype=F32)[:, None] * inv_freq[None, :]
    steps = (coarse * jnp.arange(seq_len // coarse, dtype=F32))[:, None] * inv_freq[None, :]
    both = lax.optimization_barrier((jnp.cos(fine), jnp.sin(fine), jnp.cos(steps), jnp.sin(steps)))
    cb, sb, ca, sa = both[0][None], both[1][None], both[2][:, None], both[3][:, None]
    cos = (ca * cb - sa * sb).reshape(seq_len, HD // 2)
    sin = (sa * cb + ca * sb).reshape(seq_len, HD // 2)
    return jnp.concatenate([cos, cos], -1), jnp.concatenate([-sin, sin], -1)


def qkv_kernel(x_ref, wq_ref, wk_ref, wv_ref, cos_ref, sin_ref, ln_ref, q_ref, k_ref, kt_ref, v_ref, vt_ref):
    normed, _ = normalize(x_ref[...].astype(F32))
    ln = normed.astype(BF16)
    ln_ref[...] = ln
    cos, sin = cos_ref[...], sin_ref[...]
    q, k, v = nn(ln, wq_ref[...]), nn(ln, wk_ref[...]), nn(ln, wv_ref[...]).astype(BF16)
    for h in range(q.shape[1] // HD):
        at = slice(h * HD, (h + 1) * HD)
        qh, kh = q[:, at], k[:, at]
        qr = (qh * cos + pltpu.roll(qh, HD // 2, 1) * sin) * Q_SCALE
        kr = (kh * cos + pltpu.roll(kh, HD // 2, 1) * sin).astype(BF16)
        q_ref[:, at] = qr.astype(BF16)
        k_ref[:, at] = kr
        kt_ref[at, :] = kr.T
        vt_ref[at, :] = v[:, at].T
    v_ref[...] = v


def qkv(x, w_query, w_key, w_value, cos, sin, block=256):
    rows, width = x.shape
    dim = w_query.shape[1]
    by_row = lambda n: pl.BlockSpec((block, n), lambda i: (i, 0))
    whole = pl.BlockSpec((width, dim), lambda i: (0, 0))
    flipped = pl.BlockSpec((dim, block), lambda i: (0, i))
    shape = lambda *dims: jax.ShapeDtypeStruct(dims, BF16)
    return pl.pallas_call(
        qkv_kernel,
        grid=(rows // block,),
        in_specs=[by_row(width), whole, whole, whole, by_row(HD), by_row(HD)],
        out_specs=[by_row(width), by_row(dim), by_row(dim), flipped, by_row(dim), flipped],
        out_shape=[
            shape(rows, width),
            shape(rows, dim),
            shape(rows, dim),
            shape(dim, rows),
            shape(rows, dim),
            shape(dim, rows),
        ],
        compiler_params=pltpu.CompilerParams(vmem_limit_bytes=40 << 20),
        cost_estimate=pl.CostEstimate(
            flops=6 * rows * width * dim, bytes_accessed=4 * rows * width + 6 * width * dim + 10 * rows * dim, transcendentals=0
        ),
        name="qkv",
    )(x, w_query, w_key, w_value, cos, sin)


def allowed_mask(key0, q0, shape, prefix):
    cols = key0 + lax.broadcasted_iota(jnp.int32, shape, 0)
    rows = q0 + lax.broadcasted_iota(jnp.int32, shape, 1)
    return (cols <= rows) | (cols < prefix)


def key_blocks(q0, bq, bk, prefix):
    full = jnp.maximum((q0 + 1) // bk, prefix // bk)
    total = jnp.maximum((q0 + bq + bk - 1) // bk, (prefix + bk - 1) // bk)
    return full, total


def fwd_kernel(prefix_ref, q_ref, k_ref, vt_ref, o_ref, lse_ref, m_s, l_s, acc_s, *, row0, bq, bk):
    prefix = prefix_ref[0]
    q0 = row0 + pl.program_id(1) * bq
    q = q_ref[...]
    m_s[...] = jnp.full(m_s.shape, NEG, F32)
    l_s[...] = jnp.zeros(l_s.shape, F32)
    acc_s[...] = jnp.zeros(acc_s.shape, F32)

    def step(j, masked):
        k0 = pl.multiple_of(j * bk, bk)
        s = nt(k_ref[pl.ds(k0, bk), :], q)
        if masked:
            s = jnp.where(allowed_mask(k0, q0, s.shape, prefix), s, NEG)
        m_old = m_s[...]
        m_new = jnp.maximum(m_old, jnp.max(s, 0, keepdims=True))
        p = jnp.exp2(s - m_new)
        a = jnp.exp2(m_old - m_new)
        l_s[...] = l_s[...] * a + jnp.sum(p, 0, keepdims=True)
        acc_s[...] = acc_s[...] * a + nn(vt_ref[:, pl.ds(k0, bk)], p.astype(BF16))
        m_s[...] = m_new

    full, total = key_blocks(q0, bq, bk, prefix)
    lax.fori_loop(0, full, lambda j, c: (step(j, False), c)[1], 0)
    lax.fori_loop(full, total, lambda j, c: (step(j, True), c)[1], 0)
    l = l_s[...]
    o_ref[...] = (acc_s[...] / l).T.astype(BF16)
    lse_ref[...] = (m_s[...] + jnp.log2(l))[None]


def attn_fwd(q, k, vt, prefix, row0, rows, bq=512, bk=512):
    seq, dim = k.shape
    heads = dim // HD
    bq, bk = min(bq, rows), min(bk, rows)
    first = row0 // bq
    return pl.pallas_call(
        partial(fwd_kernel, row0=row0, bq=bq, bk=bk),
        grid_spec=pltpu.PrefetchScalarGridSpec(
            num_scalar_prefetch=1,
            grid=(heads, rows // bq),
            in_specs=[
                pl.BlockSpec((bq, HD), lambda h, i, p: (i + first, h)),
                pl.BlockSpec((seq, HD), lambda h, i, p: (0, h)),
                pl.BlockSpec((HD, seq), lambda h, i, p: (h, 0)),
            ],
            out_specs=[
                pl.BlockSpec((bq, HD), lambda h, i, p: (i, h)),
                pl.BlockSpec((1, 1, bq), lambda h, i, p: (h, 0, i)),
            ],
            scratch_shapes=[
                pltpu.VMEM((1, bq), F32),
                pltpu.VMEM((1, bq), F32),
                pltpu.VMEM((HD, bq), F32),
            ],
        ),
        out_shape=[
            jax.ShapeDtypeStruct((rows, dim), BF16),
            jax.ShapeDtypeStruct((heads, 1, rows), F32),
        ],
        compiler_params=pltpu.CompilerParams(vmem_limit_bytes=32 << 20),
        cost_estimate=pl.CostEstimate(
            flops=12 * rows * seq * dim, bytes_accessed=4 * seq * dim + 4 * rows * dim, transcendentals=rows * seq * heads
        ),
        name="attn_fwd",
    )(prefix, q, k, vt)


def unrope(t, cos, sin):
    return t * cos - pltpu.roll(t, HD // 2, 1) * sin


def bwd_kernel(prefix_ref, q_ref, k_ref, kt_ref, v_ref, o_ref, do_ref, lse_ref, cq_ref, sq_ref, ck_ref, sk_ref, *rest, row0, bq, bk, keys, has_in, lo):
    rest = list(rest)
    if has_in:
        dk_in, dv_in = rest[:2]
        rest = rest[2:]
    dq_ref, dk_ref, dv_ref = rest[:3]
    rest = rest[3:]
    if lo:
        dk_part, dv_part = rest[:2]
        rest = rest[2:]
    dk_s, dv_s, dq_s = rest
    qi = pl.program_id(1)
    prefix = prefix_ref[0]
    q0 = row0 + qi * bq

    @pl.when(qi == 0)
    def _():
        if has_in:
            dk_s[...] = dk_in[...]
            dv_s[...] = dv_in[...]
        else:
            dk_s[...] = jnp.zeros(dk_s.shape, F32)
            dv_s[...] = jnp.zeros(dv_s.shape, F32)

    q, do = q_ref[...], do_ref[...]
    lse = lse_ref[0]
    delta = jnp.sum((do.astype(F32) * o_ref[...].astype(F32)).T, 0, keepdims=True)
    dq_s[...] = jnp.zeros(dq_s.shape, F32)

    def step(j, masked):
        k0 = pl.multiple_of(j * bk, bk)
        at = pl.ds(k0, bk)
        s = nt(k_ref[at, :], q)
        p = jnp.exp2(s - lse)
        if masked:
            p = jnp.where(allowed_mask(k0, q0, s.shape, prefix), p, 0.0)
        dp = nt(v_ref[at, :], do)
        ds = (p * (dp - delta)).astype(BF16)
        dv_s[at, :] += nn(p.astype(BF16), do)
        dk_s[at, :] += nn(ds, q)
        dq_s[...] += nn(kt_ref[:, at], ds)

    full, total = key_blocks(q0, bq, bk, prefix)
    lax.fori_loop(0, full, lambda j, c: (step(j, False), c)[1], 0)
    lax.fori_loop(full, total, lambda j, c: (step(j, True), c)[1], 0)
    dq_ref[...] = unrope((dq_s[...] * HD**-0.5).T, cq_ref[...], sq_ref[...]).astype(BF16)

    @pl.when(qi == pl.num_programs(1) - 1)
    def _():
        dk_ref[...] = unrope(dk_s[lo:keys, :] * (1.0 / LOG2E), ck_ref[...], sk_ref[...]).astype(BF16)
        dv_ref[...] = dv_s[lo:keys, :].astype(BF16)
        if lo:
            dk_part[...] = dk_s[:lo, :]
            dv_part[...] = dv_s[:lo, :]


def attn_bwd(q, k, kt, v, o, do, lse, cos, sin, prefix, row0, rows, lo, part=None, bq=512, bk=512):
    dim = k.shape[1]
    heads = dim // HD
    keys = row0 + rows
    own = keys - lo
    bq, bk = min(bq, rows), min(bk, rows)
    first = row0 // bq
    has_in = part is not None
    full = lambda n: pl.BlockSpec((n, HD), lambda h, i, p: (0, h))
    table_q = pl.BlockSpec((bq, HD), lambda h, i, p: (i + first, 0))
    table_k = pl.BlockSpec((own, HD), lambda h, i, p: (lo // own, 0))
    by_q = pl.BlockSpec((bq, HD), lambda h, i, p: (i, h))
    in_specs = [
        pl.BlockSpec((bq, HD), lambda h, i, p: (i + first, h)),
        full(keys),
        pl.BlockSpec((HD, keys), lambda h, i, p: (h, 0)),
        full(keys),
        by_q,
        pl.BlockSpec((bq, HD), lambda h, i, p: (i + first, h)),
        pl.BlockSpec((1, 1, bq), lambda h, i, p: (h, 0, i)),
        table_q,
        table_q,
        table_k,
        table_k,
    ]
    args = [q, k, kt, v, o, do, lse, cos, sin, cos, sin]
    if has_in:
        in_specs += [full(keys), full(keys)]
        args += list(part)
    out_specs = [by_q, full(own), full(own)]
    out_shape = [jax.ShapeDtypeStruct((rows, dim), BF16)] + [jax.ShapeDtypeStruct((own, dim), BF16)] * 2
    if lo:
        out_specs += [full(lo), full(lo)]
        out_shape += [jax.ShapeDtypeStruct((lo, dim), F32)] * 2
    return pl.pallas_call(
        partial(bwd_kernel, row0=row0, bq=bq, bk=bk, keys=keys, has_in=has_in, lo=lo),
        grid_spec=pltpu.PrefetchScalarGridSpec(
            num_scalar_prefetch=1,
            grid=(heads, rows // bq),
            in_specs=in_specs,
            out_specs=out_specs,
            scratch_shapes=[
                pltpu.VMEM((keys, HD), F32),
                pltpu.VMEM((keys, HD), F32),
                pltpu.VMEM((HD, bq), F32),
            ],
        ),
        out_shape=out_shape,
        compiler_params=pltpu.CompilerParams(vmem_limit_bytes=48 << 20),
        cost_estimate=pl.CostEstimate(
            flops=24 * rows * keys * dim, bytes_accessed=8 * keys * dim + 8 * rows * dim, transcendentals=rows * keys * heads
        ),
        name="attn_bwd",
    )(prefix, *args)


def resident(a):
    return pl.BlockSpec(a.shape, lambda *_: (0,) * a.ndim, pipeline_mode=pl.Buffered(1))


def call(kernel, grid, in_specs, out_specs, out_shape, name, flops, traffic, scratch=(), prefetch=1, vmem=56, exps=0):
    return pl.pallas_call(
        kernel,
        grid_spec=pltpu.PrefetchScalarGridSpec(
            num_scalar_prefetch=prefetch,
            grid=grid,
            in_specs=in_specs,
            out_specs=out_specs,
            scratch_shapes=list(scratch),
        ),
        out_shape=out_shape,
        compiler_params=pltpu.CompilerParams(vmem_limit_bytes=vmem << 20),
        cost_estimate=pl.CostEstimate(flops=flops, bytes_accessed=traffic, transcendentals=exps),
        name=name,
    )


def bf16(*dims):
    return jax.ShapeDtypeStruct(dims, BF16)


def by_core(at_ref, keep_ref, send_ref, value):
    ours = lax.rem(pl.program_id(0), 2) == at_ref[0]

    @pl.when(ours)
    def _():
        keep_ref[...] = value

    @pl.when(jnp.logical_not(ours))
    def _():
        send_ref[...] = value


def half_blocks(block, width):
    return [pl.BlockSpec((block, width), lambda i, a: (i // 2, 0))] * 2


def sum_nt_kernel(at_ref, *refs, terms):
    xs, ws, (keep_ref, send_ref) = refs[:terms], refs[terms : 2 * terms], refs[2 * terms :]
    total = nt(xs[0][...], ws[0][...])
    for x, w in zip(xs[1:], ws[1:]):
        total = total + nt(x[...], w[...])
    by_core(at_ref, keep_ref, send_ref, total.astype(BF16))


def sum_nt(at, xs, ws, block):
    rows = xs[0].shape[0]
    depth = sum(x.shape[1] for x in xs)
    width = ws[0].shape[0]
    return call(
        partial(sum_nt_kernel, terms=len(xs)),
        (rows // block,),
        [pl.BlockSpec((block, x.shape[1]), lambda i, a: (i, 0)) for x in xs] + [resident(w) for w in ws],
        half_blocks(block, width),
        [bf16(rows // 2, width)] * 2,
        "sum_nt",
        2 * rows * depth * width,
        2 * rows * (depth + width) + 2 * depth * width,
        vmem=40,
    )(at, *xs, *ws)


def doubling_order(chips):
    order, hop = [0], chips // 2
    while hop:
        order = order + [o ^ hop for o in order]
        hop //= 2
    return order


def ff_kernel(
    at_ref, mixed_ref, x_ref, cot_ref, wm_ref, wo_ref, wg_ref, wu_ref, wd_ref,
    res_ref, ln_ref, hid_ref, gg_ref, gu_ref, keep_ref, send_ref, mine, other, *, first,
):
    core, chip = at_ref[0], at_ref[1]
    dim = mixed_ref.shape[2]
    chips = mixed_ref.shape[0] // 2
    for j, away in enumerate(doubling_order(chips)):
        z = lax.bitwise_xor(chip, away)
        cols = slice(j * dim, (j + 1) * dim)
        mine[:, cols] = mixed_ref[2 * z + core]
        other[:, cols] = mixed_ref[2 * z + 1 - core]
    residual = x_ref[...].astype(F32) + nn(mine[...], wm_ref[...]) + nn(other[...], wo_ref[...])

    @pl.when(pl.program_id(0) + first == 2 * chip + core)
    def _():
        res_ref[...] = residual

    normed, _ = normalize(residual)
    ln = normed.astype(BF16)
    ln_ref[...] = ln
    gate = nn(ln, wg_ref[...])
    up = nn(ln, wu_ref[...])
    grad = nt(cot_ref[...], wd_ref[...])
    sig = 1.0 / (1.0 + jnp.exp(-gate))
    act = gate * sig
    hid_ref[...] = (act * up).astype(BF16)
    gg = (grad * up * sig * (1.0 + gate * (1.0 - sig))).astype(BF16)
    gu = (grad * act).astype(BF16)
    gg_ref[...] = gg
    gu_ref[...] = gu
    by_core(at_ref, keep_ref, send_ref, (nt(gg, wg_ref[...]) + nt(gu, wu_ref[...])).astype(BF16))


def feed_forward(at, mixed, x, cot, row0, w_mine, w_other, w_gate, w_up, w_down, block):
    n, rows, dim = mixed.shape
    width = x.shape[1]
    hid = w_gate.shape[1]
    first = row0 // block
    by_row = lambda n, f=0: pl.BlockSpec((block, n), lambda i, a: (i + f, 0))
    return call(
        partial(ff_kernel, first=first),
        (rows // block,),
        [
            pl.BlockSpec((n, block, dim), lambda i, a: (0, i, 0)),
            by_row(width, first),
            by_row(width, first),
            resident(w_mine),
            resident(w_other),
            resident(w_gate),
            resident(w_up),
            resident(w_down),
        ],
        [pl.BlockSpec((block, width), lambda i, a: (0, 0)), by_row(width), by_row(hid), by_row(hid), by_row(hid)]
        + half_blocks(block, width),
        [jax.ShapeDtypeStruct((block, width), F32), bf16(rows, width)]
        + [bf16(rows, hid)] * 3
        + [bf16(rows // 2, width)] * 2,
        "feed_forward",
        10 * rows * width * hid + 2 * rows * width * width,
        6 * width * hid + 2 * width * width + 10 * rows * width + 6 * rows * hid,
        scratch=[pltpu.VMEM((block, n * dim // 2), BF16)] * 2,
        exps=rows * hid,
    )(at, mixed, x, cot, w_mine, w_other, w_gate, w_up, w_down)


def ffn_out_kernel(at_ref, lo_ref, hi_ref, rlo_ref, rhi_ref, w_ref, keep_ref, send_ref, out, *, steps):
    step = pl.program_id(0)
    ours = step == 2 * at_ref[1] + at_ref[0]
    for hid_ref, res_ref, inside in ((lo_ref, rlo_ref, step < steps // 2), (hi_ref, rhi_ref, step >= steps // 2)):

        @pl.when(inside)
        def _():
            out[...] = nn(hid_ref[...], w_ref[...])

        @pl.when(jnp.logical_and(inside, ours))
        def _():
            out[...] = out[...] + res_ref[...]

    by_core(at_ref, keep_ref, send_ref, out[...].astype(BF16))


def ffn_out(at, hid_lo, hid_hi, res_lo, res_hi, w_down):
    half, hid = hid_lo.shape
    block, width = res_lo.shape
    steps = 2 * half // block
    per = steps // 2
    return call(
        partial(ffn_out_kernel, steps=steps),
        (steps,),
        [
            pl.BlockSpec((block, hid), lambda i, a: (jnp.minimum(i, per - 1), 0)),
            pl.BlockSpec((block, hid), lambda i, a: (jnp.maximum(i - per, 0), 0)),
            resident(res_lo),
            resident(res_hi),
            resident(w_down),
        ],
        half_blocks(block, width),
        [bf16(half, width)] * 2,
        "ffn_out",
        4 * half * hid * width,
        4 * half * (hid + width) + 2 * hid * width,
        scratch=[pltpu.VMEM((block, width), F32)],
        vmem=40,
    )(at, hid_lo, hid_hi, res_lo, res_hi, w_down)


def columns_kernel(dp_ref, *refs):
    pieces, out = refs[:-1], refs[-1]
    for s, piece in enumerate(pieces):

        @pl.when(lax.bitwise_xor(dp_ref[0], pl.program_id(0)) == s)
        def _():
            out[...] = piece[...]


def columns(dp, pieces):
    rows, part = pieces[0].shape
    n = len(pieces)
    return call(
        columns_kernel,
        (n,),
        [resident(p) for p in pieces],
        pl.BlockSpec((rows, part), lambda i, a: (0, i)),
        bf16(rows, n * part),
        "columns",
        0,
        4 * n * rows * part,
        vmem=40,
    )(dp, *pieces)


def block_grad_kernel(at_ref, held_ref, came_ref, rlo_ref, rhi_ref, cot_ref, wm_ref, wo_ref, grad_ref, low_ref, out_ref, *, chips):
    for res_ref, inside in ((rlo_ref, at_ref[1] < chips // 2), (rhi_ref, at_ref[1] >= chips // 2)):

        @pl.when(jnp.logical_and(pl.program_id(0) == 0, inside))
        def _():
            total = held_ref[...].astype(F32) + came_ref[...].astype(F32)
            grad = cot_ref[...].astype(F32) + norm_back(*normalize(res_ref[...]), total)
            grad_ref[...] = grad
            low_ref[...] = grad.astype(BF16)

    ours = lax.rem(pl.program_id(0), 2) == at_ref[0]

    @pl.when(ours)
    def _():
        out_ref[0] = nt(low_ref[...], wm_ref[...]).astype(BF16)

    @pl.when(jnp.logical_not(ours))
    def _():
        out_ref[0] = nt(low_ref[...], wo_ref[...]).astype(BF16)


def block_grad(at, held, came, res_lo, res_hi, cotangent, w_mine, w_other, n):
    block, width = cotangent.shape
    dim = w_mine.shape[0] * 2 // n
    one = pl.BlockSpec((block, width), lambda i, a: (0, 0))
    by_chip = pl.BlockSpec((dim, width), lambda i, a: (a[2 + i // 2], 0))
    return call(
        partial(block_grad_kernel, chips=n // 2),
        (n,),
        [one, one, one, one, one, by_chip, by_chip],
        [one, one, pl.BlockSpec((1, block, dim), lambda i, a: (i, 0, 0))],
        [jax.ShapeDtypeStruct((block, width), F32), bf16(block, width), bf16(n, block, dim)],
        "block_grad",
        2 * block * width * width,
        2 * width * width + 20 * block * width,
    )(at, held, came, res_lo, res_hi, cotangent, w_mine, w_other)


def grad_out_kernel(at_ref, mlo_ref, mhi_ref, grad_ref, keep_ref, send_ref, part, *, chips):
    for mixed_ref, inside in ((mlo_ref, at_ref[1] < chips // 2), (mhi_ref, at_ref[1] >= chips // 2)):

        @pl.when(inside)
        def _():
            part[...] = tn(mixed_ref[0], grad_ref[...]).astype(BF16)

    by_core(at_ref, keep_ref, send_ref, part[...])


def grad_out_part(at, mixed_lo, mixed_hi, grad):
    n, _, dim = mixed_lo.shape
    block, width = grad.shape
    rows = pl.BlockSpec((1, block, dim), lambda i, a: (i, lax.rem(2 * a[1] + a[0], n // 2), 0))
    return call(
        partial(grad_out_kernel, chips=n // 2),
        (n,),
        [rows, rows, resident(grad)],
        half_blocks(dim, width),
        [bf16(n // 2 * dim, width)] * 2,
        "grad_out_part",
        2 * block * n * dim * width,
        2 * n * dim * (2 * block + width),
        scratch=[pltpu.VMEM((dim, width), BF16)],
        vmem=40,
    )(at, mixed_lo, mixed_hi, grad)


def wgrad_kernel(at_ref, *refs, groups):
    out = refs[-1]
    used, col = 0, 0
    for pieces, count in groups:
        a = refs[used : used + pieces]
        used += pieces
        for _ in range(count):
            b = refs[used : used + pieces]
            used += pieces
            total = tn(a[0][...], b[0][...])
            for s in range(1, pieces):
                total = total + tn(a[s][...], b[s][...])
            out[:, col : col + total.shape[1]] = total.astype(BF16)
            col += total.shape[1]


def wgrad(at, groups, block=512):
    in_specs, args, kinds, cols, flops = [], [], [], 0, 0
    for a, bs in groups:
        for piece in a:
            array, rows, at_row = piece if isinstance(piece, tuple) else (piece, piece.shape[0], 0)
            wide = array.shape[1]
            size = min(block, wide)
            in_specs.append(pl.BlockSpec((rows, size), lambda i, g, r=at_row: (r, i)))
            args.append(array)
        for b in bs:
            for piece in b:
                array, rows, at_row = piece if isinstance(piece, tuple) else (piece, piece.shape[0], 0)
                in_specs.append(
                    pl.BlockSpec(
                        (rows, array.shape[1]), lambda i, g, r=at_row: (r, 0), pipeline_mode=pl.Buffered(1)
                    )
                )
                args.append(array)
                flops += 2 * wide * rows * array.shape[1]
            cols += array.shape[1]
        kinds.append((len(a), len(bs)))
    return call(
        partial(wgrad_kernel, groups=kinds),
        (wide // size,),
        in_specs,
        pl.BlockSpec((size, cols), lambda i, g: (i, 0)),
        bf16(wide, cols),
        "wgrad",
        flops,
        4 * wide * cols + sum(2 * x.size for x in args),
    )(at, *args)


def halve_kernel(bit_ref, a_ref, b_ref, keep_ref, send_ref):
    total = (a_ref[...].astype(F32) + b_ref[...].astype(F32)).astype(BF16)
    ours = lax.rem(pl.program_id(0), 2) == bit_ref[0]

    @pl.when(ours)
    def _():
        keep_ref[...] = total

    @pl.when(jnp.logical_not(ours))
    def _():
        send_ref[...] = total


def halve(bit, a, b):
    count, rows, width = a.shape
    one = pl.BlockSpec((1, rows, width), lambda i, s: (i, 0, 0))
    pair = pl.BlockSpec((1, rows, width), lambda i, s: (i // 2, 0, 0))
    return call(
        halve_kernel,
        (count,),
        [one, one],
        [pair, pair],
        [bf16(count // 2, rows, width)] * 2,
        "halve",
        count * rows * width,
        6 * count * rows * width,
        vmem=40,
    )(bit, a, b)


def add_kernel(at_ref, a_ref, b_ref, out_ref):
    out_ref[...] = (a_ref[...].astype(F32) + b_ref[...].astype(F32)).astype(BF16)


def add_rows(at, a, b, block=256):
    rows, width = a.shape
    one = pl.BlockSpec((block, width), lambda i, s: (i, 0))
    return call(
        add_kernel,
        (rows // block,),
        [one, one],
        one,
        bf16(rows, width),
        "add_rows",
        rows * width,
        6 * rows * width,
        vmem=40,
    )(at, a, b)


def local(layer_input, prefix_len, w_query, w_key, w_value, w_out, w_gate, w_up, w_down, cotangent):
    seq, width = layer_input.shape
    n = lax.axis_size("tensor")
    chips = n // 2
    stages = chips.bit_length() - 1
    place = lax.axis_index("tensor")
    chip, core = place // 2, lax.rem(place, 2)
    half = seq // 2
    block = seq // n
    found = [doubling_order(chips).index(z) for z in range(chips)]
    at = jnp.concatenate([jnp.stack([core, chip]), jnp.array(found)[lax.bitwise_xor(chip, jnp.arange(chips))]])
    at = at.astype(jnp.int32)
    latest = [None]

    def done(value):
        latest[0] = value
        return value

    def later(value):
        if latest[0] is None:
            return value
        return lax.optimization_barrier((value, latest[0]))[0]

    def start(x, pairs):
        return lax.ppermute(later(x), "tensor", pairs)

    swap_cores = [(t, t ^ 1) for t in range(n)]

    def chips_apart(hop):
        return [(t, t ^ (2 * hop)) for t in range(n)]

    class Scatter:
        def __init__(self, keep, sent, blocks, hop=1):
            self.held = keep.reshape(blocks, -1, keep.shape[-1])
            self.hop = hop
            if sent is None:
                self.split()
            else:
                self.coming = start(sent, swap_cores).reshape(self.held.shape)

        def split(self):
            bit = lax.rem(chip // self.hop, 2)
            pairs = self.held.reshape(self.held.shape[0] // 2, 2, -1, self.held.shape[-1])
            self.held = lax.dynamic_index_in_dim(pairs, bit, 1, False)
            self.sent = done(lax.dynamic_index_in_dim(pairs, 1 - bit, 1, False))

        def add(self):
            bit = lax.rem(chip // self.hop, 2).astype(jnp.int32)[None]
            self.held, self.sent = halve(bit, self.held, later(self.coming))
            done(self.sent)

        def send(self):
            self.coming = start(self.sent, chips_apart(self.hop))
            self.hop *= 2

        def step(self):
            self.add()
            self.send()

        def last(self):
            return self.held[0], later(self.coming)[0]

        def total(self):
            held, came = self.last()
            return held.astype(F32) + came.astype(F32)

    def half_sum(name, key):
        s = halves[name][key]
        halves[name]["sum"] = done(add_rows(at, s.held[0], later(s.coming)[0]))

    def across():
        upper = chip >= chips // 2
        sums = [later(halves[h]["sum"]) for h in ("lo", "hi")]
        kept = jnp.where(upper, sums[1], sums[0])
        sent = done(jnp.where(upper, sums[0], sums[1]))
        return kept, lax.ppermute(sent, "tensor", chips_apart(chips // 2))

    starts = {"hi": half, "lo": 0}
    hi, lo = {}, {}
    halves = {"hi": hi, "lo": lo}

    def attention(name):
        c = halves[name]
        c["mixed"], c["lse"] = attn_fwd(later(q), k, vt, prefix_len, starts[name], half)
        done(c["mixed"])

    def spread(name):
        c = halves[name]
        c["all_mixed"] = lax.all_gather(later(c["mixed"]), "tensor")

    def both_ways(name):
        c = halves[name]
        c["residual"], c["ln"], c["hidden"], c["g_gate"], c["g_up"], c["keep"], c["send"] = feed_forward(
            at, later(c["all_mixed"]), layer_input, cot, starts[name], *w_full, w_gate, w_up, w_down, block
        )
        done(c["keep"])

    part = None

    def attention_back(name):
        nonlocal part
        c = halves[name]
        first = starts[name]
        grads = attn_bwd(q, k, kt, v, c["mixed"], g_mixed, c["lse"], cos, sin, prefix_len, first, half, first, part)
        c["dq"], c["dk"], c["dv"] = grads[:3]
        part = grads[3:]
        done(c["dq"])
        c["keep"], c["send"] = sum_nt(at, [c["dq"], c["dk"], c["dv"]], [w_query, w_key, w_value], block)
        done(c["keep"])

    def to_dp(grad, dim):
        return lax.psum_scatter(grad, "dp", scatter_dimension=dim, tiled=True)

    own = chips // 2

    def rest(transfer):
        for _ in range(stages - 2):
            transfer.step()

    n_dp = lax.axis_size("dp")
    dp_place = lax.axis_index("dp")
    piece = lax.dynamic_slice_in_dim(w_out, dp_place * (width // n_dp), width // n_dp, 1)
    hop = chips // 2
    coming = start(piece, chips_apart(hop))
    cot = lax.all_gather(cotangent, "tensor", axis=0, tiled=True)
    cos, sin = rope_tables(seq)
    done(cos)
    piece = jnp.concatenate([piece, later(coming)], 0)
    first = True
    while hop > 1:
        hop //= 2
        coming = start(done(piece), chips_apart(hop))
        if first:
            ln_one, q, k, kt, v, vt = qkv(layer_input, w_query, w_key, w_value, later(cos), sin)
            done(q)
            attention("hi")
            first = False
        piece = jnp.concatenate([piece, later(coming)], 0)
    pieces = [done(piece)] + [lax.ppermute(piece, "dp", [(d, d ^ s) for d in range(n_dp)]) for s in range(1, n_dp)]
    spread("hi")
    attention("lo")
    w_mine = done(columns(dp_place.astype(jnp.int32)[None], [later(p) for p in pieces]))
    w_full = [w_mine, lax.ppermute(w_mine, "tensor", swap_cores)]
    spread("lo")
    cot = done(later(cot))
    both_ways("hi")
    hi["g_norm"] = Scatter(hi["keep"], hi["send"], own)
    hi["g_norm"].step()
    both_ways("lo")
    rest(hi["g_norm"])
    half_sum("hi", "g_norm")
    lo["g_norm"] = Scatter(lo["keep"], lo["send"], own)
    lo["g_norm"].step()
    grad_gate_up = done(
        wgrad(at, [([hi["ln"], later(lo["ln"])], [[hi["g_gate"], lo["g_gate"]], [hi["g_up"], lo["g_up"]]])])
    )
    rest(lo["g_norm"])
    half_sum("lo", "g_norm")
    grad_gate_up = to_dp(later(grad_gate_up), 0)
    kept, came = across()
    grad_down = done(wgrad(at, [([hi["hidden"], later(lo["hidden"])], [[(cot, half, 1), (cot, half, 0)]])]))
    keep, sent = ffn_out(at, later(lo["hidden"]), hi["hidden"], lo["residual"], hi["residual"], w_down)
    done(keep)
    came = done(later(came))
    grad_down = to_dp(later(grad_down), 1)
    ffn = Scatter(keep, sent, chips)
    g_res, g_res_low, by_head = block_grad(
        at, kept, later(came), lo["residual"], hi["residual"], cotangent, *w_full, n
    )
    out_keep, out_sent = grad_out_part(at, lo["all_mixed"], hi["all_mixed"], done(g_res_low))
    done(out_keep)
    ffn.add()
    g_mixed = lax.all_to_all(later(by_head), "tensor", 0, 0, tiled=True).reshape(seq, -1)
    out_came = start(out_sent, swap_cores)
    ffn.send()
    grad_out = done(add_rows(at, out_keep, later(out_came)))
    g_mixed = done(later(g_mixed))
    grad_out = to_dp(later(grad_out), 1)
    attention_back("hi")
    ffn.add()
    hi["g_one"] = Scatter(hi["keep"], hi["send"], own)
    ffn.send()
    hi["g_one"].step()
    attention_back("lo")
    rest(hi["g_one"])
    half_sum("hi", "g_one")
    lo["g_one"] = Scatter(lo["keep"], lo["send"], own)
    lo["g_one"].step()
    rows = ln_one.shape[0] // 2
    grads = done(
        wgrad(
            at, [([(later(ln_one), rows, 0), (ln_one, rows, 1)], [[lo[key], hi[key]] for key in ("dq", "dk", "dv")])]
        )
    )
    grad_gate_up = done(later(grad_gate_up).astype(F32))
    rest(ffn)
    layer_output = done(ffn.total())
    rest(lo["g_one"])
    half_sum("lo", "g_one")
    grads = to_dp(later(grads), 0)
    grad_down = done(later(grad_down).astype(F32))
    out_sum = Scatter(later(grad_out), None, chips)
    kept, came = across()
    out_sum.send()
    for _ in range(stages - 1):
        out_sum.step()
    back = kept.astype(F32) + later(came).astype(F32)
    normed, inv = normalize(lax.dynamic_slice_in_dim(layer_input, place * block, block, 0).astype(F32))
    input_grad = done(g_res + norm_back(normed, inv, back))
    grad_out = done(out_sum.total())
    grads = later(grads).astype(F32)
    hid, dim = w_gate.shape[1], w_query.shape[1]
    return (
        layer_output,
        input_grad,
        grads[:, :dim],
        grads[:, dim : 2 * dim],
        grads[:, 2 * dim :],
        grad_out,
        grad_gate_up[:, :hid],
        grad_gate_up[:, hid:],
        grad_down,
    )


def solution(mesh):
    in_specs = (
        P("dp", None),
        P("dp"),
        P(None, "tensor"),
        P(None, "tensor"),
        P(None, "tensor"),
        P("tensor", None),
        P(None, "tensor"),
        P(None, "tensor"),
        P("tensor", None),
        P(("dp", "tensor"), None),
    )
    out_specs = (
        P(("dp", "tensor"), None),
        P(("dp", "tensor"), None),
        P("dp", "tensor"),
        P("dp", "tensor"),
        P("dp", "tensor"),
        P("tensor", "dp"),
        P("dp", "tensor"),
        P("dp", "tensor"),
        P("tensor", "dp"),
    )
    return jax.shard_map(local, mesh=mesh, in_specs=in_specs, out_specs=out_specs, check_vma=False)
```

```python
import math
from functools import partial

import jax
import jax.numpy as jnp
from jax import lax
from jax.experimental import pallas as pl
from jax.experimental.pallas import tpu as pltpu
from jax.sharding import PartitionSpec as P

HD = 128
EPS = 1e-05
ROPE_BASE = 10000.0
NEG = -1e30
LOG2E = math.log2(math.e)
Q_SCALE = LOG2E * HD**-0.5
F32 = jnp.float32
BF16 = jnp.bfloat16


def nt(a, b):
    return lax.dot_general(a, b, (((1,), (1,)), ((), ())), preferred_element_type=F32)


def nn(a, b):
    return lax.dot_general(a, b, (((1,), (0,)), ((), ())), preferred_element_type=F32)


def tn(a, b):
    return lax.dot_general(a, b, (((0,), (0,)), ((), ())), preferred_element_type=F32)


def normalize(values):
    centered = values - jnp.mean(values, -1, keepdims=True)
    inv_std = lax.rsqrt(jnp.mean(centered * centered, -1, keepdims=True) + EPS)
    return centered * inv_std, inv_std


def norm_back(normed, inv_std, upstream):
    first_mean = jnp.mean(upstream, -1, keepdims=True)
    second_mean = jnp.mean(upstream * normed, -1, keepdims=True)
    return inv_std * (upstream - first_mean - normed * second_mean)


def rope_tables(seq_len, coarse=64):
    inv_freq = ROPE_BASE ** (-(2.0 * jnp.arange(HD // 2, dtype=F32)) / HD)
    fine = jnp.arange(coarse, dtype=F32)[:, None] * inv_freq[None, :]
    steps = (coarse * jnp.arange(seq_len // coarse, dtype=F32))[:, None] * inv_freq[None, :]
    both = lax.optimization_barrier((jnp.cos(fine), jnp.sin(fine), jnp.cos(steps), jnp.sin(steps)))
    cb, sb, ca, sa = both[0][None], both[1][None], both[2][:, None], both[3][:, None]
    cos = (ca * cb - sa * sb).reshape(seq_len, HD // 2)
    sin = (sa * cb + ca * sb).reshape(seq_len, HD // 2)
    return jnp.concatenate([cos, cos], -1), jnp.concatenate([-sin, sin], -1)


def qkv_kernel(x_ref, wq_ref, wk_ref, wv_ref, cos_ref, sin_ref, ln_ref, q_ref, k_ref, kt_ref, v_ref, vt_ref):
    normed, _ = normalize(x_ref[...].astype(F32))
    ln = normed.astype(BF16)
    ln_ref[...] = ln
    cos, sin = cos_ref[...], sin_ref[...]
    q, k, v = nn(ln, wq_ref[...]), nn(ln, wk_ref[...]), nn(ln, wv_ref[...]).astype(BF16)
    for h in range(q.shape[1] // HD):
        at = slice(h * HD, (h + 1) * HD)
        qh, kh = q[:, at], k[:, at]
        qr = (qh * cos + pltpu.roll(qh, HD // 2, 1) * sin) * Q_SCALE
        kr = (kh * cos + pltpu.roll(kh, HD // 2, 1) * sin).astype(BF16)
        q_ref[:, at] = qr.astype(BF16)
        k_ref[:, at] = kr
        kt_ref[at, :] = kr.T
        vt_ref[at, :] = v[:, at].T
    v_ref[...] = v


def qkv(x, w_query, w_key, w_value, cos, sin, block=256):
    rows, width = x.shape
    dim = w_query.shape[1]
    by_row = lambda n: pl.BlockSpec((block, n), lambda i: (i, 0))
    whole = pl.BlockSpec((width, dim), lambda i: (0, 0))
    flipped = pl.BlockSpec((dim, block), lambda i: (0, i))
    shape = lambda *dims: jax.ShapeDtypeStruct(dims, BF16)
    return pl.pallas_call(
        qkv_kernel,
        grid=(rows // block,),
        in_specs=[by_row(width), whole, whole, whole, by_row(HD), by_row(HD)],
        out_specs=[by_row(width), by_row(dim), by_row(dim), flipped, by_row(dim), flipped],
        out_shape=[
            shape(rows, width),
            shape(rows, dim),
            shape(rows, dim),
            shape(dim, rows),
            shape(rows, dim),
            shape(dim, rows),
        ],
        compiler_params=pltpu.CompilerParams(vmem_limit_bytes=40 << 20),
        cost_estimate=pl.CostEstimate(
            flops=6 * rows * width * dim, bytes_accessed=4 * rows * width + 6 * width * dim + 10 * rows * dim, transcendentals=0
        ),
        name="qkv",
    )(x, w_query, w_key, w_value, cos, sin)


def allowed_mask(key0, q0, shape, prefix):
    cols = key0 + lax.broadcasted_iota(jnp.int32, shape, 0)
    rows = q0 + lax.broadcasted_iota(jnp.int32, shape, 1)
    return (cols <= rows) | (cols < prefix)


def key_blocks(q0, bq, bk, prefix):
    full = jnp.maximum((q0 + 1) // bk, prefix // bk)
    total = jnp.maximum((q0 + bq + bk - 1) // bk, (prefix + bk - 1) // bk)
    return full, total


def fwd_kernel(prefix_ref, q_ref, k_ref, vt_ref, o_ref, lse_ref, m_s, l_s, acc_s, *, row0, bq, bk):
    prefix = prefix_ref[0]
    q0 = row0 + pl.program_id(1) * bq
    q = q_ref[...]
    m_s[...] = jnp.full(m_s.shape, NEG, F32)
    l_s[...] = jnp.zeros(l_s.shape, F32)
    acc_s[...] = jnp.zeros(acc_s.shape, F32)

    def step(j, masked):
        k0 = pl.multiple_of(j * bk, bk)
        s = nt(k_ref[pl.ds(k0, bk), :], q)
        if masked:
            s = jnp.where(allowed_mask(k0, q0, s.shape, prefix), s, NEG)
        m_old = m_s[...]
        m_new = jnp.maximum(m_old, jnp.max(s, 0, keepdims=True))
        p = jnp.exp2(s - m_new)
        a = jnp.exp2(m_old - m_new)
        l_s[...] = l_s[...] * a + jnp.sum(p, 0, keepdims=True)
        acc_s[...] = acc_s[...] * a + nn(vt_ref[:, pl.ds(k0, bk)], p.astype(BF16))
        m_s[...] = m_new

    full, total = key_blocks(q0, bq, bk, prefix)
    lax.fori_loop(0, full, lambda j, c: (step(j, False), c)[1], 0)
    lax.fori_loop(full, total, lambda j, c: (step(j, True), c)[1], 0)
    l = l_s[...]
    o_ref[...] = (acc_s[...] / l).T.astype(BF16)
    lse_ref[...] = (m_s[...] + jnp.log2(l))[None]


def attn_fwd(q, k, vt, prefix, row0, rows, bq=512, bk=512):
    seq, dim = k.shape
    heads = dim // HD
    bq, bk = min(bq, rows), min(bk, rows)
    first = row0 // bq
    return pl.pallas_call(
        partial(fwd_kernel, row0=row0, bq=bq, bk=bk),
        grid_spec=pltpu.PrefetchScalarGridSpec(
            num_scalar_prefetch=1,
            grid=(heads, rows // bq),
            in_specs=[
                pl.BlockSpec((bq, HD), lambda h, i, p: (i + first, h)),
                pl.BlockSpec((seq, HD), lambda h, i, p: (0, h)),
                pl.BlockSpec((HD, seq), lambda h, i, p: (h, 0)),
            ],
            out_specs=[
                pl.BlockSpec((bq, HD), lambda h, i, p: (i, h)),
                pl.BlockSpec((1, 1, bq), lambda h, i, p: (h, 0, i)),
            ],
            scratch_shapes=[
                pltpu.VMEM((1, bq), F32),
                pltpu.VMEM((1, bq), F32),
                pltpu.VMEM((HD, bq), F32),
            ],
        ),
        out_shape=[
            jax.ShapeDtypeStruct((rows, dim), BF16),
            jax.ShapeDtypeStruct((heads, 1, rows), F32),
        ],
        compiler_params=pltpu.CompilerParams(vmem_limit_bytes=32 << 20),
        cost_estimate=pl.CostEstimate(
            flops=12 * rows * seq * dim, bytes_accessed=4 * seq * dim + 4 * rows * dim, transcendentals=rows * seq * heads
        ),
        name="attn_fwd",
    )(prefix, q, k, vt)


def unrope(t, cos, sin):
    return t * cos - pltpu.roll(t, HD // 2, 1) * sin


def bwd_kernel(prefix_ref, q_ref, k_ref, kt_ref, v_ref, o_ref, do_ref, lse_ref, cq_ref, sq_ref, ck_ref, sk_ref, *rest, row0, bq, bk, keys, has_in, lo):
    rest = list(rest)
    if has_in:
        dk_in, dv_in = rest[:2]
        rest = rest[2:]
    dq_ref, dk_ref, dv_ref = rest[:3]
    rest = rest[3:]
    if lo:
        dk_part, dv_part = rest[:2]
        rest = rest[2:]
    dk_s, dv_s, dq_s = rest
    qi = pl.program_id(1)
    prefix = prefix_ref[0]
    q0 = row0 + qi * bq

    @pl.when(qi == 0)
    def _():
        if has_in:
            dk_s[...] = dk_in[...]
            dv_s[...] = dv_in[...]
        else:
            dk_s[...] = jnp.zeros(dk_s.shape, F32)
            dv_s[...] = jnp.zeros(dv_s.shape, F32)

    q, do = q_ref[...], do_ref[...]
    lse = lse_ref[0]
    delta = jnp.sum((do.astype(F32) * o_ref[...].astype(F32)).T, 0, keepdims=True)
    dq_s[...] = jnp.zeros(dq_s.shape, F32)

    def step(j, masked):
        k0 = pl.multiple_of(j * bk, bk)
        at = pl.ds(k0, bk)
        s = nt(k_ref[at, :], q)
        p = jnp.exp2(s - lse)
        if masked:
            p = jnp.where(allowed_mask(k0, q0, s.shape, prefix), p, 0.0)
        dp = nt(v_ref[at, :], do)
        ds = (p * (dp - delta)).astype(BF16)
        dv_s[at, :] += nn(p.astype(BF16), do)
        dk_s[at, :] += nn(ds, q)
        dq_s[...] += nn(kt_ref[:, at], ds)

    full, total = key_blocks(q0, bq, bk, prefix)
    lax.fori_loop(0, full, lambda j, c: (step(j, False), c)[1], 0)
    lax.fori_loop(full, total, lambda j, c: (step(j, True), c)[1], 0)
    dq_ref[...] = unrope((dq_s[...] * HD**-0.5).T, cq_ref[...], sq_ref[...]).astype(BF16)

    @pl.when(qi == pl.num_programs(1) - 1)
    def _():
        dk_ref[...] = unrope(dk_s[lo:keys, :] * (1.0 / LOG2E), ck_ref[...], sk_ref[...]).astype(BF16)
        dv_ref[...] = dv_s[lo:keys, :].astype(BF16)
        if lo:
            dk_part[...] = dk_s[:lo, :]
            dv_part[...] = dv_s[:lo, :]


def attn_bwd(q, k, kt, v, o, do, lse, cos, sin, prefix, row0, rows, lo, part=None, bq=512, bk=512):
    dim = k.shape[1]
    heads = dim // HD
    keys = row0 + rows
    own = keys - lo
    bq, bk = min(bq, rows), min(bk, rows)
    first = row0 // bq
    has_in = part is not None
    full = lambda n: pl.BlockSpec((n, HD), lambda h, i, p: (0, h))
    table_q = pl.BlockSpec((bq, HD), lambda h, i, p: (i + first, 0))
    table_k = pl.BlockSpec((own, HD), lambda h, i, p: (lo // own, 0))
    by_q = pl.BlockSpec((bq, HD), lambda h, i, p: (i, h))
    in_specs = [
        pl.BlockSpec((bq, HD), lambda h, i, p: (i + first, h)),
        full(keys),
        pl.BlockSpec((HD, keys), lambda h, i, p: (h, 0)),
        full(keys),
        by_q,
        pl.BlockSpec((bq, HD), lambda h, i, p: (i + first, h)),
        pl.BlockSpec((1, 1, bq), lambda h, i, p: (h, 0, i)),
        table_q,
        table_q,
        table_k,
        table_k,
    ]
    args = [q, k, kt, v, o, do, lse, cos, sin, cos, sin]
    if has_in:
        in_specs += [full(keys), full(keys)]
        args += list(part)
    out_specs = [by_q, full(own), full(own)]
    out_shape = [jax.ShapeDtypeStruct((rows, dim), BF16)] + [jax.ShapeDtypeStruct((own, dim), BF16)] * 2
    if lo:
        out_specs += [full(lo), full(lo)]
        out_shape += [jax.ShapeDtypeStruct((lo, dim), F32)] * 2
    return pl.pallas_call(
        partial(bwd_kernel, row0=row0, bq=bq, bk=bk, keys=keys, has_in=has_in, lo=lo),
        grid_spec=pltpu.PrefetchScalarGridSpec(
            num_scalar_prefetch=1,
            grid=(heads, rows // bq),
            in_specs=in_specs,
            out_specs=out_specs,
            scratch_shapes=[
                pltpu.VMEM((keys, HD), F32),
                pltpu.VMEM((keys, HD), F32),
                pltpu.VMEM((HD, bq), F32),
            ],
        ),
        out_shape=out_shape,
        compiler_params=pltpu.CompilerParams(vmem_limit_bytes=48 << 20),
        cost_estimate=pl.CostEstimate(
            flops=24 * rows * keys * dim, bytes_accessed=8 * keys * dim + 8 * rows * dim, transcendentals=rows * keys * heads
        ),
        name="attn_bwd",
    )(prefix, *args)


def resident(a):
    return pl.BlockSpec(a.shape, lambda *_: (0,) * a.ndim, pipeline_mode=pl.Buffered(1))


def call(kernel, grid, in_specs, out_specs, out_shape, name, flops, traffic, scratch=(), prefetch=1, vmem=56, exps=0):
    return pl.pallas_call(
        kernel,
        grid_spec=pltpu.PrefetchScalarGridSpec(
            num_scalar_prefetch=prefetch,
            grid=grid,
            in_specs=in_specs,
            out_specs=out_specs,
            scratch_shapes=list(scratch),
        ),
        out_shape=out_shape,
        compiler_params=pltpu.CompilerParams(vmem_limit_bytes=vmem << 20),
        cost_estimate=pl.CostEstimate(flops=flops, bytes_accessed=traffic, transcendentals=exps),
        name=name,
    )


def bf16(*dims):
    return jax.ShapeDtypeStruct(dims, BF16)


def by_core(at_ref, keep_ref, send_ref, value):
    ours = lax.rem(pl.program_id(0), 2) == at_ref[0]

    @pl.when(ours)
    def _():
        keep_ref[...] = value

    @pl.when(jnp.logical_not(ours))
    def _():
        send_ref[...] = value


def half_blocks(block, width):
    return [pl.BlockSpec((block, width), lambda i, a: (i // 2, 0))] * 2


def sum_nt_kernel(at_ref, *refs, terms):
    xs, ws, (keep_ref, send_ref) = refs[:terms], refs[terms : 2 * terms], refs[2 * terms :]
    total = nt(xs[0][...], ws[0][...])
    for x, w in zip(xs[1:], ws[1:]):
        total = total + nt(x[...], w[...])
    by_core(at_ref, keep_ref, send_ref, total.astype(BF16))


def sum_nt(at, xs, ws, block):
    rows = xs[0].shape[0]
    depth = sum(x.shape[1] for x in xs)
    width = ws[0].shape[0]
    return call(
        partial(sum_nt_kernel, terms=len(xs)),
        (rows // block,),
        [pl.BlockSpec((block, x.shape[1]), lambda i, a: (i, 0)) for x in xs] + [resident(w) for w in ws],
        half_blocks(block, width),
        [bf16(rows // 2, width)] * 2,
        "sum_nt",
        2 * rows * depth * width,
        2 * rows * (depth + width) + 2 * depth * width,
        vmem=40,
    )(at, *xs, *ws)


def doubling_order(chips):
    order, hop = [0], chips // 2
    while hop:
        order = order + [o ^ hop for o in order]
        hop //= 2
    return order


def ff_kernel(
    at_ref, mixed_ref, x_ref, cot_ref, wm_any, wo_any, wg_any, wu_any, wd_any,
    res_ref, ln_ref, hid_ref, gg_ref, gu_ref, keep_ref, send_ref,
    mine, other, wm_ref, wo_ref, wg_ref, wu_ref, wd_ref, sems, *, first,
):
    core, chip = at_ref[0], at_ref[1]
    dim = mixed_ref.shape[2]
    weights = ((wm_any, wm_ref), (wo_any, wo_ref), (wg_any, wg_ref), (wu_any, wu_ref), (wd_any, wd_ref))
    copies = [pltpu.make_async_copy(source, held, sems.at[s]) for s, (source, held) in enumerate(weights)]

    @pl.when(pl.program_id(0) == 0)
    def _():
        for copy in copies:
            copy.start()

    def need(s):
        @pl.when(pl.program_id(0) == 0)
        def _():
            copies[s].wait()

    chips = mixed_ref.shape[0] // 2
    for j, away in enumerate(doubling_order(chips)):
        z = lax.bitwise_xor(chip, away)
        cols = slice(j * dim, (j + 1) * dim)
        mine[:, cols] = mixed_ref[2 * z + core]
        other[:, cols] = mixed_ref[2 * z + 1 - core]
    need(0)
    residual = x_ref[...].astype(F32) + nn(mine[...], wm_ref[...])
    need(1)
    residual = residual + nn(other[...], wo_ref[...])

    @pl.when(pl.program_id(0) + first == 2 * chip + core)
    def _():
        res_ref[...] = residual

    normed, _ = normalize(residual)
    ln = normed.astype(BF16)
    ln_ref[...] = ln
    need(2)
    gate = nn(ln, wg_ref[...])
    need(3)
    up = nn(ln, wu_ref[...])
    need(4)
    grad = nt(cot_ref[...], wd_ref[...])
    sig = 1.0 / (1.0 + jnp.exp(-gate))
    act = gate * sig
    hid_ref[...] = (act * up).astype(BF16)
    gg = (grad * up * sig * (1.0 + gate * (1.0 - sig))).astype(BF16)
    gu = (grad * act).astype(BF16)
    gg_ref[...] = gg
    gu_ref[...] = gu
    by_core(at_ref, keep_ref, send_ref, (nt(gg, wg_ref[...]) + nt(gu, wu_ref[...])).astype(BF16))


def feed_forward(at, mixed, x, cot, row0, w_mine, w_other, w_gate, w_up, w_down, block):
    n, rows, dim = mixed.shape
    width = x.shape[1]
    hid = w_gate.shape[1]
    first = row0 // block
    by_row = lambda n, f=0: pl.BlockSpec((block, n), lambda i, a: (i + f, 0))
    return call(
        partial(ff_kernel, first=first),
        (rows // block,),
        [
            pl.BlockSpec((n, block, dim), lambda i, a: (0, i, 0)),
            by_row(width, first),
            by_row(width, first),
        ]
        + [pl.BlockSpec(memory_space=pl.ANY)] * 5,
        [pl.BlockSpec((block, width), lambda i, a: (0, 0)), by_row(width), by_row(hid), by_row(hid), by_row(hid)]
        + half_blocks(block, width),
        [jax.ShapeDtypeStruct((block, width), F32), bf16(rows, width)]
        + [bf16(rows, hid)] * 3
        + [bf16(rows // 2, width)] * 2,
        "feed_forward",
        10 * rows * width * hid + 2 * rows * width * width,
        6 * width * hid + 2 * width * width + 10 * rows * width + 6 * rows * hid,
        scratch=[pltpu.VMEM((block, n * dim // 2), BF16)] * 2
        + [pltpu.VMEM(w.shape, BF16) for w in (w_mine, w_other, w_gate, w_up, w_down)]
        + [pltpu.SemaphoreType.DMA((5,))],
        exps=rows * hid,
    )(at, mixed, x, cot, w_mine, w_other, w_gate, w_up, w_down)


def ffn_out_kernel(at_ref, lo_ref, hi_ref, rlo_ref, rhi_ref, w_ref, keep_ref, send_ref, out, *, steps):
    step = pl.program_id(0)
    ours = step == 2 * at_ref[1] + at_ref[0]
    for hid_ref, res_ref, inside in ((lo_ref, rlo_ref, step < steps // 2), (hi_ref, rhi_ref, step >= steps // 2)):

        @pl.when(inside)
        def _():
            out[...] = nn(hid_ref[...], w_ref[...])

        @pl.when(jnp.logical_and(inside, ours))
        def _():
            out[...] = out[...] + res_ref[...]

    by_core(at_ref, keep_ref, send_ref, out[...].astype(BF16))


def ffn_out(at, hid_lo, hid_hi, res_lo, res_hi, w_down):
    half, hid = hid_lo.shape
    block, width = res_lo.shape
    steps = 2 * half // block
    per = steps // 2
    return call(
        partial(ffn_out_kernel, steps=steps),
        (steps,),
        [
            pl.BlockSpec((block, hid), lambda i, a: (jnp.minimum(i, per - 1), 0)),
            pl.BlockSpec((block, hid), lambda i, a: (jnp.maximum(i - per, 0), 0)),
            resident(res_lo),
            resident(res_hi),
            resident(w_down),
        ],
        half_blocks(block, width),
        [bf16(half, width)] * 2,
        "ffn_out",
        4 * half * hid * width,
        4 * half * (hid + width) + 2 * hid * width,
        scratch=[pltpu.VMEM((block, width), F32)],
        vmem=40,
    )(at, hid_lo, hid_hi, res_lo, res_hi, w_down)


def columns_kernel(dp_ref, *refs):
    pieces, out = refs[:-1], refs[-1]
    for s, piece in enumerate(pieces):

        @pl.when(lax.bitwise_xor(dp_ref[0], pl.program_id(0)) == s)
        def _():
            out[...] = piece[...]


def columns(dp, pieces):
    rows, part = pieces[0].shape
    n = len(pieces)
    return call(
        columns_kernel,
        (n,),
        [resident(p) for p in pieces],
        pl.BlockSpec((rows, part), lambda i, a: (0, i)),
        bf16(rows, n * part),
        "columns",
        0,
        4 * n * rows * part,
        vmem=40,
    )(dp, *pieces)


def block_grad_kernel(at_ref, held_ref, came_ref, rlo_ref, rhi_ref, cot_ref, wm_ref, wo_ref, grad_ref, low_ref, out_ref, *, chips):
    for res_ref, inside in ((rlo_ref, at_ref[1] < chips // 2), (rhi_ref, at_ref[1] >= chips // 2)):

        @pl.when(jnp.logical_and(pl.program_id(0) == 0, inside))
        def _():
            total = held_ref[...].astype(F32) + came_ref[...].astype(F32)
            grad = cot_ref[...].astype(F32) + norm_back(*normalize(res_ref[...]), total)
            grad_ref[...] = grad
            low_ref[...] = grad.astype(BF16)

    ours = lax.rem(pl.program_id(0), 2) == at_ref[0]

    @pl.when(ours)
    def _():
        out_ref[0] = nt(low_ref[...], wm_ref[...]).astype(BF16)

    @pl.when(jnp.logical_not(ours))
    def _():
        out_ref[0] = nt(low_ref[...], wo_ref[...]).astype(BF16)


def block_grad(at, held, came, res_lo, res_hi, cotangent, w_mine, w_other, n):
    block, width = cotangent.shape
    dim = w_mine.shape[0] * 2 // n
    one = pl.BlockSpec((block, width), lambda i, a: (0, 0))
    by_chip = pl.BlockSpec((dim, width), lambda i, a: (a[2 + i // 2], 0))
    return call(
        partial(block_grad_kernel, chips=n // 2),
        (n,),
        [one, one, one, one, one, by_chip, by_chip],
        [one, one, pl.BlockSpec((1, block, dim), lambda i, a: (i, 0, 0))],
        [jax.ShapeDtypeStruct((block, width), F32), bf16(block, width), bf16(n, block, dim)],
        "block_grad",
        2 * block * width * width,
        2 * width * width + 20 * block * width,
    )(at, held, came, res_lo, res_hi, cotangent, w_mine, w_other)


def grad_out_kernel(at_ref, mlo_ref, mhi_ref, own_ref, came_ref, out_ref, both, *, chips):
    block = own_ref.shape[0]
    core = at_ref[0]

    @pl.when(pl.program_id(0) == 0)
    def _():
        both[pl.ds(pl.multiple_of(core * block, block), block), :] = own_ref[...]
        both[pl.ds(pl.multiple_of((1 - core) * block, block), block), :] = came_ref[...]

    for mixed_ref, inside in ((mlo_ref, at_ref[1] < chips // 2), (mhi_ref, at_ref[1] >= chips // 2)):

        @pl.when(inside)
        def _():
            out_ref[...] = tn(mixed_ref[0], both[...]).astype(BF16)


def grad_out_part(at, mixed_lo, mixed_hi, own, came):
    n, _, dim = mixed_lo.shape
    block, width = own.shape
    chips = n // 2
    rows = pl.BlockSpec((1, 2 * block, dim), lambda i, a: (2 * i + a[0], lax.rem(a[1], chips // 2), 0))
    return call(
        partial(grad_out_kernel, chips=chips),
        (chips,),
        [rows, rows, resident(own), resident(came)],
        pl.BlockSpec((dim, width), lambda i, a: (i, 0)),
        bf16(chips * dim, width),
        "grad_out_part",
        4 * block * chips * dim * width,
        2 * chips * dim * (4 * block + width),
        scratch=[pltpu.VMEM((2 * block, width), BF16)],
        vmem=40,
    )(at, mixed_lo, mixed_hi, own, came)


def wgrad_kernel(at_ref, *refs, groups):
    out = refs[-1]
    used, col = 0, 0
    for pieces, count in groups:
        a = refs[used : used + pieces]
        used += pieces
        for _ in range(count):
            b = refs[used : used + pieces]
            used += pieces
            total = tn(a[0][...], b[0][...])
            for s in range(1, pieces):
                total = total + tn(a[s][...], b[s][...])
            out[:, col : col + total.shape[1]] = total.astype(BF16)
            col += total.shape[1]


def wgrad(at, groups, block=512):
    in_specs, args, kinds, cols, flops = [], [], [], 0, 0
    for a, bs in groups:
        for piece in a:
            array, rows, at_row = piece if isinstance(piece, tuple) else (piece, piece.shape[0], 0)
            wide = array.shape[1]
            size = min(block, wide)
            in_specs.append(pl.BlockSpec((rows, size), lambda i, g, r=at_row: (r, i)))
            args.append(array)
        for b in bs:
            for piece in b:
                array, rows, at_row = piece if isinstance(piece, tuple) else (piece, piece.shape[0], 0)
                in_specs.append(
                    pl.BlockSpec(
                        (rows, array.shape[1]), lambda i, g, r=at_row: (r, 0), pipeline_mode=pl.Buffered(1)
                    )
                )
                args.append(array)
                flops += 2 * wide * rows * array.shape[1]
            cols += array.shape[1]
        kinds.append((len(a), len(bs)))
    return call(
        partial(wgrad_kernel, groups=kinds),
        (wide // size,),
        in_specs,
        pl.BlockSpec((size, cols), lambda i, g: (i, 0)),
        bf16(wide, cols),
        "wgrad",
        flops,
        4 * wide * cols + sum(2 * x.size for x in args),
    )(at, *args)


def halve_kernel(bit_ref, a_ref, b_ref, keep_ref, send_ref):
    total = (a_ref[...].astype(F32) + b_ref[...].astype(F32)).astype(BF16)
    ours = lax.rem(pl.program_id(0), 2) == bit_ref[0]

    @pl.when(ours)
    def _():
        keep_ref[...] = total

    @pl.when(jnp.logical_not(ours))
    def _():
        send_ref[...] = total


def halve(bit, a, b):
    count, rows, width = a.shape
    one = pl.BlockSpec((1, rows, width), lambda i, s: (i, 0, 0))
    pair = pl.BlockSpec((1, rows, width), lambda i, s: (i // 2, 0, 0))
    return call(
        halve_kernel,
        (count,),
        [one, one],
        [pair, pair],
        [bf16(count // 2, rows, width)] * 2,
        "halve",
        count * rows * width,
        6 * count * rows * width,
        vmem=40,
    )(bit, a, b)


def add_kernel(at_ref, a_ref, b_ref, out_ref):
    out_ref[...] = (a_ref[...].astype(F32) + b_ref[...].astype(F32)).astype(BF16)


def add_rows(at, a, b, block=256):
    rows, width = a.shape
    one = pl.BlockSpec((block, width), lambda i, s: (i, 0))
    return call(
        add_kernel,
        (rows // block,),
        [one, one],
        one,
        bf16(rows, width),
        "add_rows",
        rows * width,
        6 * rows * width,
        vmem=40,
    )(at, a, b)


def local(layer_input, prefix_len, w_query, w_key, w_value, w_out, w_gate, w_up, w_down, cotangent):
    seq, width = layer_input.shape
    n = lax.axis_size("tensor")
    chips = n // 2
    stages = chips.bit_length() - 1
    place = lax.axis_index("tensor")
    chip, core = place // 2, lax.rem(place, 2)
    half = seq // 2
    block = seq // n
    found = [doubling_order(chips).index(z) for z in range(chips)]
    at = jnp.concatenate([jnp.stack([core, chip]), jnp.array(found)[lax.bitwise_xor(chip, jnp.arange(chips))]])
    at = at.astype(jnp.int32)
    latest = [None]

    def done(value):
        latest[0] = value
        return value

    def later(value):
        if latest[0] is None:
            return value
        return lax.optimization_barrier((value, latest[0]))[0]

    def start(x, pairs):
        return lax.ppermute(later(x), "tensor", pairs)

    swap_cores = [(t, t ^ 1) for t in range(n)]

    def chips_apart(hop):
        return [(t, t ^ (2 * hop)) for t in range(n)]

    class Scatter:
        def __init__(self, keep, sent, blocks, hop=1):
            self.held = keep.reshape(blocks, -1, keep.shape[-1])
            self.hop = hop
            if sent is None:
                self.split()
            else:
                self.coming = start(sent, swap_cores).reshape(self.held.shape)

        def split(self):
            bit = lax.rem(chip // self.hop, 2)
            pairs = self.held.reshape(self.held.shape[0] // 2, 2, -1, self.held.shape[-1])
            self.held = lax.dynamic_index_in_dim(pairs, bit, 1, False)
            self.sent = done(lax.dynamic_index_in_dim(pairs, 1 - bit, 1, False))

        def add(self):
            bit = lax.rem(chip // self.hop, 2).astype(jnp.int32)[None]
            self.held, self.sent = halve(bit, self.held, later(self.coming))
            done(self.sent)

        def send(self):
            self.coming = start(self.sent, chips_apart(self.hop))
            self.hop *= 2

        def step(self):
            self.add()
            self.send()

        def last(self):
            return self.held[0], later(self.coming)[0]

        def total(self):
            held, came = self.last()
            return held.astype(F32) + came.astype(F32)

    def half_sum(name, key):
        s = halves[name][key]
        halves[name]["sum"] = done(add_rows(at, s.held[0], later(s.coming)[0]))

    def across():
        upper = chip >= chips // 2
        sums = [later(halves[h]["sum"]) for h in ("lo", "hi")]
        kept = jnp.where(upper, sums[1], sums[0])
        sent = done(jnp.where(upper, sums[0], sums[1]))
        return kept, lax.ppermute(sent, "tensor", chips_apart(chips // 2))

    starts = {"hi": half, "lo": 0}
    hi, lo = {}, {}
    halves = {"hi": hi, "lo": lo}

    def attention(name):
        c = halves[name]
        c["mixed"], c["lse"] = attn_fwd(later(q), k, vt, prefix_len, starts[name], half)
        done(c["mixed"])

    def spread(name):
        c = halves[name]
        c["all_mixed"] = lax.all_gather(later(c["mixed"]), "tensor")

    def both_ways(name):
        c = halves[name]
        c["residual"], c["ln"], c["hidden"], c["g_gate"], c["g_up"], c["keep"], c["send"] = feed_forward(
            at, later(c["all_mixed"]), layer_input, cot, starts[name], *w_full, w_gate, w_up, w_down, block
        )
        done(c["keep"])

    part = None

    def attention_back(name):
        nonlocal part
        c = halves[name]
        first = starts[name]
        grads = attn_bwd(q, k, kt, v, c["mixed"], g_mixed, c["lse"], cos, sin, prefix_len, first, half, first, part)
        c["dq"], c["dk"], c["dv"] = grads[:3]
        part = grads[3:]
        done(c["dq"])
        c["keep"], c["send"] = sum_nt(at, [c["dq"], c["dk"], c["dv"]], [w_query, w_key, w_value], block)
        done(c["keep"])

    def to_dp(grad, dim):
        return lax.psum_scatter(grad, "dp", scatter_dimension=dim, tiled=True)

    own = chips // 2

    def rest(transfer):
        for _ in range(stages - 2):
            transfer.step()

    n_dp = lax.axis_size("dp")
    dp_place = lax.axis_index("dp")
    piece = lax.dynamic_slice_in_dim(w_out, dp_place * (width // n_dp), width // n_dp, 1)
    hop = chips // 2
    coming = start(piece, chips_apart(hop))
    cot = lax.all_gather(cotangent, "tensor", axis=0, tiled=True)
    cos, sin = rope_tables(seq)
    done(cos)
    piece = jnp.concatenate([piece, later(coming)], 0)
    first = True
    while hop > 1:
        hop //= 2
        coming = start(done(piece), chips_apart(hop))
        if first:
            ln_one, q, k, kt, v, vt = qkv(layer_input, w_query, w_key, w_value, later(cos), sin)
            done(q)
            attention("hi")
            first = False
        piece = jnp.concatenate([piece, later(coming)], 0)
    pieces = [done(piece)] + [lax.ppermute(piece, "dp", [(d, d ^ s) for d in range(n_dp)]) for s in range(1, n_dp)]
    spread("hi")
    attention("lo")
    w_mine = done(columns(dp_place.astype(jnp.int32)[None], [later(p) for p in pieces]))
    w_full = [w_mine, lax.ppermute(w_mine, "tensor", swap_cores)]
    spread("lo")
    cot = done(later(cot))
    both_ways("hi")
    hi["g_norm"] = Scatter(hi["keep"], hi["send"], own)
    hi["g_norm"].step()
    both_ways("lo")
    rest(hi["g_norm"])
    half_sum("hi", "g_norm")
    lo["g_norm"] = Scatter(lo["keep"], lo["send"], own)
    lo["g_norm"].step()
    grad_gate_up = done(
        wgrad(at, [([hi["ln"], later(lo["ln"])], [[hi["g_gate"], lo["g_gate"]], [hi["g_up"], lo["g_up"]]])])
    )
    rest(lo["g_norm"])
    half_sum("lo", "g_norm")
    grad_gate_up = to_dp(later(grad_gate_up), 0)
    kept, came = across()
    grad_down = done(wgrad(at, [([hi["hidden"], later(lo["hidden"])], [[(cot, half, 1), (cot, half, 0)]])]))
    keep, sent = ffn_out(at, later(lo["hidden"]), hi["hidden"], lo["residual"], hi["residual"], w_down)
    done(keep)
    came = done(later(came))
    grad_down = to_dp(later(grad_down), 1)
    ffn = Scatter(keep, sent, chips)
    g_res, g_res_low, by_head = block_grad(
        at, kept, later(came), lo["residual"], hi["residual"], cotangent, *w_full, n
    )
    g_mixed = lax.all_to_all(done(by_head), "tensor", 0, 0, tiled=True).reshape(seq, -1)
    g_came = start(g_res_low, swap_cores)
    ffn.add()
    g_came = done(later(g_came))
    ffn.send()
    grad_out = done(grad_out_part(at, lo["all_mixed"], hi["all_mixed"], g_res_low, later(g_came)))
    g_mixed = done(later(g_mixed))
    attention_back("hi")
    g_mixed = later(g_mixed)
    attention_back("lo")
    ffn.add()
    grad_out = to_dp(later(grad_out), 1)
    ffn.send()
    hi["g_one"] = Scatter(hi["keep"], hi["send"], own)
    lo["g_one"] = Scatter(lo["keep"], lo["send"], own)
    hi["g_one"].step()
    lo["g_one"].step()
    rows = ln_one.shape[0] // 2
    grads = done(
        wgrad(
            at, [([(later(ln_one), rows, 0), (ln_one, rows, 1)], [[lo[key], hi[key]] for key in ("dq", "dk", "dv")])]
        )
    )
    rest(hi["g_one"])
    half_sum("hi", "g_one")
    grad_gate_up = done(later(grad_gate_up).astype(F32))
    rest(ffn)
    layer_output = done(ffn.total())
    rest(lo["g_one"])
    half_sum("lo", "g_one")
    grads = to_dp(later(grads), 0)
    grad_down = done(later(grad_down).astype(F32))
    out_sum = Scatter(later(grad_out), None, chips)
    kept, came = across()
    out_sum.send()
    for _ in range(stages - 1):
        out_sum.step()
    grads = done(later(grads).astype(F32))
    back = kept.astype(F32) + later(came).astype(F32)
    normed, inv = normalize(lax.dynamic_slice_in_dim(layer_input, place * block, block, 0).astype(F32))
    input_grad = done(g_res + norm_back(normed, inv, back))
    grad_out = done(out_sum.total())
    hid, dim = w_gate.shape[1], w_query.shape[1]
    return (
        layer_output,
        input_grad,
        grads[:, :dim],
        grads[:, dim : 2 * dim],
        grads[:, 2 * dim :],
        grad_out,
        grad_gate_up[:, :hid],
        grad_gate_up[:, hid:],
        grad_down,
    )


def solution(mesh):
    in_specs = (
        P("dp", None),
        P("dp"),
        P(None, "tensor"),
        P(None, "tensor"),
        P(None, "tensor"),
        P("tensor", None),
        P(None, "tensor"),
        P(None, "tensor"),
        P("tensor", None),
        P(("dp", "tensor"), None),
    )
    out_specs = (
        P(("dp", "tensor"), None),
        P(("dp", "tensor"), None),
        P("dp", "tensor"),
        P("dp", "tensor"),
        P("dp", "tensor"),
        P("tensor", "dp"),
        P("dp", "tensor"),
        P("dp", "tensor"),
        P("tensor", "dp"),
    )
    return jax.shard_map(local, mesh=mesh, in_specs=in_specs, out_specs=out_specs, check_vma=False)
```

```python
import math
from functools import partial

import jax
import jax.numpy as jnp
from jax import lax
from jax.experimental import pallas as pl
from jax.experimental.pallas import tpu as pltpu
from jax.sharding import PartitionSpec as P

HD = 128
EPS = 1e-05
ROPE_BASE = 10000.0
NEG = -1e30
LOG2E = math.log2(math.e)
Q_SCALE = LOG2E * HD**-0.5
F32 = jnp.float32
BF16 = jnp.bfloat16


def nt(a, b):
    return lax.dot_general(a, b, (((1,), (1,)), ((), ())), preferred_element_type=F32)


def nn(a, b):
    return lax.dot_general(a, b, (((1,), (0,)), ((), ())), preferred_element_type=F32)


def tn(a, b):
    return lax.dot_general(a, b, (((0,), (0,)), ((), ())), preferred_element_type=F32)


def normalize(values):
    centered = values - jnp.mean(values, -1, keepdims=True)
    inv_std = lax.rsqrt(jnp.mean(centered * centered, -1, keepdims=True) + EPS)
    return centered * inv_std, inv_std


def norm_back(normed, inv_std, upstream):
    first_mean = jnp.mean(upstream, -1, keepdims=True)
    second_mean = jnp.mean(upstream * normed, -1, keepdims=True)
    return inv_std * (upstream - first_mean - normed * second_mean)


def rope_tables(seq_len, coarse=64):
    inv_freq = ROPE_BASE ** (-(2.0 * jnp.arange(HD // 2, dtype=F32)) / HD)
    fine = jnp.arange(coarse, dtype=F32)[:, None] * inv_freq[None, :]
    steps = (coarse * jnp.arange(seq_len // coarse, dtype=F32))[:, None] * inv_freq[None, :]
    both = lax.optimization_barrier((jnp.cos(fine), jnp.sin(fine), jnp.cos(steps), jnp.sin(steps)))
    cb, sb, ca, sa = both[0][None], both[1][None], both[2][:, None], both[3][:, None]
    cos = (ca * cb - sa * sb).reshape(seq_len, HD // 2)
    sin = (sa * cb + ca * sb).reshape(seq_len, HD // 2)
    return jnp.concatenate([cos, cos], -1), jnp.concatenate([-sin, sin], -1)


def qkv_kernel(x_ref, wq_ref, wk_ref, wv_ref, cos_ref, sin_ref, ln_ref, q_ref, k_ref, kt_ref, v_ref, vt_ref):
    normed, _ = normalize(x_ref[...].astype(F32))
    ln = normed.astype(BF16)
    ln_ref[...] = ln
    cos, sin = cos_ref[...], sin_ref[...]
    q, k, v = nn(ln, wq_ref[...]), nn(ln, wk_ref[...]), nn(ln, wv_ref[...]).astype(BF16)
    for h in range(q.shape[1] // HD):
        at = slice(h * HD, (h + 1) * HD)
        qh, kh = q[:, at], k[:, at]
        qr = (qh * cos + pltpu.roll(qh, HD // 2, 1) * sin) * Q_SCALE
        kr = (kh * cos + pltpu.roll(kh, HD // 2, 1) * sin).astype(BF16)
        q_ref[:, at] = qr.astype(BF16)
        k_ref[:, at] = kr
        kt_ref[at, :] = kr.T
        vt_ref[at, :] = v[:, at].T
    v_ref[...] = v


def qkv(x, w_query, w_key, w_value, cos, sin, block=256):
    rows, width = x.shape
    dim = w_query.shape[1]
    by_row = lambda n: pl.BlockSpec((block, n), lambda i: (i, 0))
    whole = pl.BlockSpec((width, dim), lambda i: (0, 0))
    flipped = pl.BlockSpec((dim, block), lambda i: (0, i))
    shape = lambda *dims: jax.ShapeDtypeStruct(dims, BF16)
    return pl.pallas_call(
        qkv_kernel,
        grid=(rows // block,),
        in_specs=[by_row(width), whole, whole, whole, by_row(HD), by_row(HD)],
        out_specs=[by_row(width), by_row(dim), by_row(dim), flipped, by_row(dim), flipped],
        out_shape=[
            shape(rows, width),
            shape(rows, dim),
            shape(rows, dim),
            shape(dim, rows),
            shape(rows, dim),
            shape(dim, rows),
        ],
        compiler_params=pltpu.CompilerParams(vmem_limit_bytes=40 << 20),
        cost_estimate=pl.CostEstimate(
            flops=6 * rows * width * dim, bytes_accessed=4 * rows * width + 6 * width * dim + 10 * rows * dim, transcendentals=0
        ),
        name="qkv",
    )(x, w_query, w_key, w_value, cos, sin)


def allowed_mask(key0, q0, shape, prefix):
    cols = key0 + lax.broadcasted_iota(jnp.int32, shape, 0)
    rows = q0 + lax.broadcasted_iota(jnp.int32, shape, 1)
    return (cols <= rows) | (cols < prefix)


def key_blocks(q0, bq, bk, prefix):
    full = jnp.maximum((q0 + 1) // bk, prefix // bk)
    total = jnp.maximum((q0 + bq + bk - 1) // bk, (prefix + bk - 1) // bk)
    return full, total


def fwd_kernel(prefix_ref, q_ref, k_ref, vt_ref, o_ref, lse_ref, m_s, l_s, acc_s, *, row0, bq, bk):
    prefix = prefix_ref[0]
    q0 = row0 + pl.program_id(1) * bq
    q = q_ref[...]
    m_s[...] = jnp.full(m_s.shape, NEG, F32)
    l_s[...] = jnp.zeros(l_s.shape, F32)
    acc_s[...] = jnp.zeros(acc_s.shape, F32)

    def step(j, masked):
        k0 = pl.multiple_of(j * bk, bk)
        s = nt(k_ref[pl.ds(k0, bk), :], q)
        if masked:
            s = jnp.where(allowed_mask(k0, q0, s.shape, prefix), s, NEG)
        m_old = m_s[...]
        m_new = jnp.maximum(m_old, jnp.max(s, 0, keepdims=True))
        p = jnp.exp2(s - m_new)
        a = jnp.exp2(m_old - m_new)
        l_s[...] = l_s[...] * a + jnp.sum(p, 0, keepdims=True)
        acc_s[...] = acc_s[...] * a + nn(vt_ref[:, pl.ds(k0, bk)], p.astype(BF16))
        m_s[...] = m_new

    full, total = key_blocks(q0, bq, bk, prefix)
    lax.fori_loop(0, full, lambda j, c: (step(j, False), c)[1], 0)
    lax.fori_loop(full, total, lambda j, c: (step(j, True), c)[1], 0)
    l = l_s[...]
    o_ref[...] = (acc_s[...] / l).T.astype(BF16)
    lse_ref[...] = (m_s[...] + jnp.log2(l))[None]


def attn_fwd(q, k, vt, prefix, row0, rows, bq=512, bk=512):
    seq, dim = k.shape
    heads = dim // HD
    bq, bk = min(bq, rows), min(bk, rows)
    first = row0 // bq
    return pl.pallas_call(
        partial(fwd_kernel, row0=row0, bq=bq, bk=bk),
        grid_spec=pltpu.PrefetchScalarGridSpec(
            num_scalar_prefetch=1,
            grid=(heads, rows // bq),
            in_specs=[
                pl.BlockSpec((bq, HD), lambda h, i, p: (i + first, h)),
                pl.BlockSpec((seq, HD), lambda h, i, p: (0, h)),
                pl.BlockSpec((HD, seq), lambda h, i, p: (h, 0)),
            ],
            out_specs=[
                pl.BlockSpec((bq, HD), lambda h, i, p: (i, h)),
                pl.BlockSpec((1, 1, bq), lambda h, i, p: (h, 0, i)),
            ],
            scratch_shapes=[
                pltpu.VMEM((1, bq), F32),
                pltpu.VMEM((1, bq), F32),
                pltpu.VMEM((HD, bq), F32),
            ],
        ),
        out_shape=[
            jax.ShapeDtypeStruct((rows, dim), BF16),
            jax.ShapeDtypeStruct((heads, 1, rows), F32),
        ],
        compiler_params=pltpu.CompilerParams(vmem_limit_bytes=32 << 20),
        cost_estimate=pl.CostEstimate(
            flops=12 * rows * seq * dim, bytes_accessed=4 * seq * dim + 4 * rows * dim, transcendentals=rows * seq * heads
        ),
        name="attn_fwd",
    )(prefix, q, k, vt)


def unrope(t, cos, sin):
    return t * cos - pltpu.roll(t, HD // 2, 1) * sin


def bwd_kernel(prefix_ref, q_ref, k_ref, kt_ref, v_ref, o_ref, do_ref, lse_ref, cq_ref, sq_ref, ck_ref, sk_ref, *rest, row0, bq, bk, keys, has_in, lo):
    rest = list(rest)
    if has_in:
        dk_in, dv_in = rest[:2]
        rest = rest[2:]
    dq_ref, dk_ref, dv_ref = rest[:3]
    rest = rest[3:]
    if lo:
        dk_part, dv_part = rest[:2]
        rest = rest[2:]
    dk_s, dv_s, dq_s = rest
    qi = pl.program_id(1)
    prefix = prefix_ref[0]
    q0 = row0 + qi * bq

    @pl.when(qi == 0)
    def _():
        if has_in:
            dk_s[...] = dk_in[...]
            dv_s[...] = dv_in[...]
        else:
            dk_s[...] = jnp.zeros(dk_s.shape, F32)
            dv_s[...] = jnp.zeros(dv_s.shape, F32)

    q, do = q_ref[...], do_ref[...]
    lse = lse_ref[0]
    delta = jnp.sum((do.astype(F32) * o_ref[...].astype(F32)).T, 0, keepdims=True)
    dq_s[...] = jnp.zeros(dq_s.shape, F32)

    def step(j, masked):
        k0 = pl.multiple_of(j * bk, bk)
        at = pl.ds(k0, bk)
        s = nt(k_ref[at, :], q)
        p = jnp.exp2(s - lse)
        if masked:
            p = jnp.where(allowed_mask(k0, q0, s.shape, prefix), p, 0.0)
        dp = nt(v_ref[at, :], do)
        ds = (p * (dp - delta)).astype(BF16)
        dv_s[at, :] += nn(p.astype(BF16), do)
        dk_s[at, :] += nn(ds, q)
        dq_s[...] += nn(kt_ref[:, at], ds)

    full, total = key_blocks(q0, bq, bk, prefix)
    lax.fori_loop(0, full, lambda j, c: (step(j, False), c)[1], 0)
    lax.fori_loop(full, total, lambda j, c: (step(j, True), c)[1], 0)
    dq_ref[...] = unrope((dq_s[...] * HD**-0.5).T, cq_ref[...], sq_ref[...]).astype(BF16)

    @pl.when(qi == pl.num_programs(1) - 1)
    def _():
        dk_ref[...] = unrope(dk_s[lo:keys, :] * (1.0 / LOG2E), ck_ref[...], sk_ref[...]).astype(BF16)
        dv_ref[...] = dv_s[lo:keys, :].astype(BF16)
        if lo:
            dk_part[...] = dk_s[:lo, :]
            dv_part[...] = dv_s[:lo, :]


def attn_bwd(q, k, kt, v, o, do, lse, cos, sin, prefix, row0, rows, lo, part=None, bq=512, bk=512):
    dim = k.shape[1]
    heads = dim // HD
    keys = row0 + rows
    own = keys - lo
    bq, bk = min(bq, rows), min(bk, rows)
    first = row0 // bq
    has_in = part is not None
    full = lambda n: pl.BlockSpec((n, HD), lambda h, i, p: (0, h))
    table_q = pl.BlockSpec((bq, HD), lambda h, i, p: (i + first, 0))
    table_k = pl.BlockSpec((own, HD), lambda h, i, p: (lo // own, 0))
    by_q = pl.BlockSpec((bq, HD), lambda h, i, p: (i, h))
    in_specs = [
        pl.BlockSpec((bq, HD), lambda h, i, p: (i + first, h)),
        full(keys),
        pl.BlockSpec((HD, keys), lambda h, i, p: (h, 0)),
        full(keys),
        by_q,
        pl.BlockSpec((bq, HD), lambda h, i, p: (i + first, h)),
        pl.BlockSpec((1, 1, bq), lambda h, i, p: (h, 0, i)),
        table_q,
        table_q,
        table_k,
        table_k,
    ]
    args = [q, k, kt, v, o, do, lse, cos, sin, cos, sin]
    if has_in:
        in_specs += [full(keys), full(keys)]
        args += list(part)
    out_specs = [by_q, full(own), full(own)]
    out_shape = [jax.ShapeDtypeStruct((rows, dim), BF16)] + [jax.ShapeDtypeStruct((own, dim), BF16)] * 2
    if lo:
        out_specs += [full(lo), full(lo)]
        out_shape += [jax.ShapeDtypeStruct((lo, dim), F32)] * 2
    return pl.pallas_call(
        partial(bwd_kernel, row0=row0, bq=bq, bk=bk, keys=keys, has_in=has_in, lo=lo),
        grid_spec=pltpu.PrefetchScalarGridSpec(
            num_scalar_prefetch=1,
            grid=(heads, rows // bq),
            in_specs=in_specs,
            out_specs=out_specs,
            scratch_shapes=[
                pltpu.VMEM((keys, HD), F32),
                pltpu.VMEM((keys, HD), F32),
                pltpu.VMEM((HD, bq), F32),
            ],
        ),
        out_shape=out_shape,
        compiler_params=pltpu.CompilerParams(vmem_limit_bytes=48 << 20),
        cost_estimate=pl.CostEstimate(
            flops=24 * rows * keys * dim, bytes_accessed=8 * keys * dim + 8 * rows * dim, transcendentals=rows * keys * heads
        ),
        name="attn_bwd",
    )(prefix, *args)


def resident(a):
    return pl.BlockSpec(a.shape, lambda *_: (0,) * a.ndim, pipeline_mode=pl.Buffered(1))


def call(kernel, grid, in_specs, out_specs, out_shape, name, flops, traffic, scratch=(), prefetch=1, vmem=56, exps=0):
    return pl.pallas_call(
        kernel,
        grid_spec=pltpu.PrefetchScalarGridSpec(
            num_scalar_prefetch=prefetch,
            grid=grid,
            in_specs=in_specs,
            out_specs=out_specs,
            scratch_shapes=list(scratch),
        ),
        out_shape=out_shape,
        compiler_params=pltpu.CompilerParams(vmem_limit_bytes=vmem << 20),
        cost_estimate=pl.CostEstimate(flops=flops, bytes_accessed=traffic, transcendentals=exps),
        name=name,
    )


def bf16(*dims):
    return jax.ShapeDtypeStruct(dims, BF16)


def by_core(at_ref, keep_ref, send_ref, value):
    ours = lax.rem(pl.program_id(0), 2) == at_ref[0]

    @pl.when(ours)
    def _():
        keep_ref[...] = value

    @pl.when(jnp.logical_not(ours))
    def _():
        send_ref[...] = value


def half_blocks(block, width):
    return [pl.BlockSpec((block, width), lambda i, a: (i // 2, 0))] * 2


def sum_nt_kernel(at_ref, *refs, terms):
    xs, ws, (keep_ref, send_ref) = refs[:terms], refs[terms : 2 * terms], refs[2 * terms :]
    total = nt(xs[0][...], ws[0][...])
    for x, w in zip(xs[1:], ws[1:]):
        total = total + nt(x[...], w[...])
    by_core(at_ref, keep_ref, send_ref, total.astype(BF16))


def sum_nt(at, xs, ws, block):
    rows = xs[0].shape[0]
    depth = sum(x.shape[1] for x in xs)
    width = ws[0].shape[0]
    return call(
        partial(sum_nt_kernel, terms=len(xs)),
        (rows // block,),
        [pl.BlockSpec((block, x.shape[1]), lambda i, a: (i, 0)) for x in xs] + [resident(w) for w in ws],
        half_blocks(block, width),
        [bf16(rows // 2, width)] * 2,
        "sum_nt",
        2 * rows * depth * width,
        2 * rows * (depth + width) + 2 * depth * width,
        vmem=40,
    )(at, *xs, *ws)


def doubling_order(chips):
    order, hop = [0], chips // 2
    while hop:
        order = order + [o ^ hop for o in order]
        hop //= 2
    return order


def ff_kernel(
    at_ref, mixed_ref, x_ref, cot_ref, wm_any, wo_any, wg_any, wu_any, wd_any,
    res_ref, ln_ref, hid_ref, gg_ref, gu_ref, keep_ref, send_ref,
    mine, other, wm_ref, wo_ref, wg_ref, wu_ref, wd_ref, sems, *, first,
):
    core, chip = at_ref[0], at_ref[1]
    dim = mixed_ref.shape[2]
    weights = ((wm_any, wm_ref), (wo_any, wo_ref), (wg_any, wg_ref), (wu_any, wu_ref), (wd_any, wd_ref))
    copies = [pltpu.make_async_copy(source, held, sems.at[s]) for s, (source, held) in enumerate(weights)]

    @pl.when(pl.program_id(0) == 0)
    def _():
        for copy in copies:
            copy.start()

    def need(s):
        @pl.when(pl.program_id(0) == 0)
        def _():
            copies[s].wait()

    chips = mixed_ref.shape[0] // 2
    for j, away in enumerate(doubling_order(chips)):
        z = lax.bitwise_xor(chip, away)
        cols = slice(j * dim, (j + 1) * dim)
        mine[:, cols] = mixed_ref[2 * z + core]
        other[:, cols] = mixed_ref[2 * z + 1 - core]
    need(0)
    residual = x_ref[...].astype(F32) + nn(mine[...], wm_ref[...])
    need(1)
    residual = residual + nn(other[...], wo_ref[...])

    @pl.when(pl.program_id(0) + first == 2 * chip + core)
    def _():
        res_ref[...] = residual

    normed, _ = normalize(residual)
    ln = normed.astype(BF16)
    ln_ref[...] = ln
    need(2)
    gate = nn(ln, wg_ref[...])
    need(3)
    up = nn(ln, wu_ref[...])
    need(4)
    grad = nt(cot_ref[...], wd_ref[...])
    sig = 1.0 / (1.0 + jnp.exp(-gate))
    act = gate * sig
    hid_ref[...] = (act * up).astype(BF16)
    gg = (grad * up * sig * (1.0 + gate * (1.0 - sig))).astype(BF16)
    gu = (grad * act).astype(BF16)
    gg_ref[...] = gg
    gu_ref[...] = gu
    by_core(at_ref, keep_ref, send_ref, (nt(gg, wg_ref[...]) + nt(gu, wu_ref[...])).astype(BF16))


def feed_forward(at, mixed, x, cot, row0, w_mine, w_other, w_gate, w_up, w_down, block):
    n, rows, dim = mixed.shape
    width = x.shape[1]
    hid = w_gate.shape[1]
    first = row0 // block
    by_row = lambda n, f=0: pl.BlockSpec((block, n), lambda i, a: (i + f, 0))
    return call(
        partial(ff_kernel, first=first),
        (rows // block,),
        [
            pl.BlockSpec((n, block, dim), lambda i, a: (0, i, 0)),
            by_row(width, first),
            by_row(width, first),
        ]
        + [pl.BlockSpec(memory_space=pl.ANY)] * 5,
        [pl.BlockSpec((block, width), lambda i, a: (0, 0)), by_row(width), by_row(hid), by_row(hid), by_row(hid)]
        + half_blocks(block, width),
        [jax.ShapeDtypeStruct((block, width), F32), bf16(rows, width)]
        + [bf16(rows, hid)] * 3
        + [bf16(rows // 2, width)] * 2,
        "feed_forward",
        10 * rows * width * hid + 2 * rows * width * width,
        6 * width * hid + 2 * width * width + 10 * rows * width + 6 * rows * hid,
        scratch=[pltpu.VMEM((block, n * dim // 2), BF16)] * 2
        + [pltpu.VMEM(w.shape, BF16) for w in (w_mine, w_other, w_gate, w_up, w_down)]
        + [pltpu.SemaphoreType.DMA((5,))],
        exps=rows * hid,
    )(at, mixed, x, cot, w_mine, w_other, w_gate, w_up, w_down)


def ffn_out_kernel(at_ref, lo_ref, hi_ref, rlo_ref, rhi_ref, w_ref, keep_ref, send_ref, out, *, steps):
    step = pl.program_id(0)
    ours = step == 2 * at_ref[1] + at_ref[0]
    for hid_ref, res_ref, inside in ((lo_ref, rlo_ref, step < steps // 2), (hi_ref, rhi_ref, step >= steps // 2)):

        @pl.when(inside)
        def _():
            out[...] = nn(hid_ref[...], w_ref[...])

        @pl.when(jnp.logical_and(inside, ours))
        def _():
            out[...] = out[...] + res_ref[...]

    by_core(at_ref, keep_ref, send_ref, out[...].astype(BF16))


def ffn_out(at, hid_lo, hid_hi, res_lo, res_hi, w_down):
    half, hid = hid_lo.shape
    block, width = res_lo.shape
    steps = 2 * half // block
    per = steps // 2
    return call(
        partial(ffn_out_kernel, steps=steps),
        (steps,),
        [
            pl.BlockSpec((block, hid), lambda i, a: (jnp.minimum(i, per - 1), 0)),
            pl.BlockSpec((block, hid), lambda i, a: (jnp.maximum(i - per, 0), 0)),
            resident(res_lo),
            resident(res_hi),
            resident(w_down),
        ],
        half_blocks(block, width),
        [bf16(half, width)] * 2,
        "ffn_out",
        4 * half * hid * width,
        4 * half * (hid + width) + 2 * hid * width,
        scratch=[pltpu.VMEM((block, width), F32)],
        vmem=40,
    )(at, hid_lo, hid_hi, res_lo, res_hi, w_down)


def columns_kernel(dp_ref, *refs):
    pieces, out = refs[:-1], refs[-1]
    for s, piece in enumerate(pieces):

        @pl.when(lax.bitwise_xor(dp_ref[0], pl.program_id(0)) == s)
        def _():
            out[...] = piece[...]


def columns(dp, pieces):
    rows, part = pieces[0].shape
    n = len(pieces)
    return call(
        columns_kernel,
        (n,),
        [resident(p) for p in pieces],
        pl.BlockSpec((rows, part), lambda i, a: (0, i)),
        bf16(rows, n * part),
        "columns",
        0,
        4 * n * rows * part,
        vmem=40,
    )(dp, *pieces)


def block_grad_kernel(at_ref, held_ref, came_ref, rlo_ref, rhi_ref, cot_ref, wm_ref, wo_ref, grad_ref, low_ref, out_ref, *, chips):
    for res_ref, inside in ((rlo_ref, at_ref[1] < chips // 2), (rhi_ref, at_ref[1] >= chips // 2)):

        @pl.when(jnp.logical_and(pl.program_id(0) == 0, inside))
        def _():
            total = held_ref[...].astype(F32) + came_ref[...].astype(F32)
            grad = cot_ref[...].astype(F32) + norm_back(*normalize(res_ref[...]), total)
            grad_ref[...] = grad
            low_ref[...] = grad.astype(BF16)

    ours = lax.rem(pl.program_id(0), 2) == at_ref[0]

    @pl.when(ours)
    def _():
        out_ref[0] = nt(low_ref[...], wm_ref[...]).astype(BF16)

    @pl.when(jnp.logical_not(ours))
    def _():
        out_ref[0] = nt(low_ref[...], wo_ref[...]).astype(BF16)


def block_grad(at, held, came, res_lo, res_hi, cotangent, w_mine, w_other, n):
    block, width = cotangent.shape
    dim = w_mine.shape[0] * 2 // n
    one = pl.BlockSpec((block, width), lambda i, a: (0, 0))
    by_chip = pl.BlockSpec((dim, width), lambda i, a: (a[2 + i // 2], 0))
    return call(
        partial(block_grad_kernel, chips=n // 2),
        (n,),
        [one, one, one, one, one, by_chip, by_chip],
        [one, one, pl.BlockSpec((1, block, dim), lambda i, a: (i, 0, 0))],
        [jax.ShapeDtypeStruct((block, width), F32), bf16(block, width), bf16(n, block, dim)],
        "block_grad",
        2 * block * width * width,
        2 * width * width + 20 * block * width,
    )(at, held, came, res_lo, res_hi, cotangent, w_mine, w_other)


def grad_out_kernel(at_ref, mlo_ref, mhi_ref, own_ref, came_ref, out_ref, both, *, chips):
    block = own_ref.shape[0]
    core = at_ref[0]

    @pl.when(pl.program_id(0) == 0)
    def _():
        both[pl.ds(pl.multiple_of(core * block, block), block), :] = own_ref[...]
        both[pl.ds(pl.multiple_of((1 - core) * block, block), block), :] = came_ref[...]

    for mixed_ref, inside in ((mlo_ref, at_ref[1] < chips // 2), (mhi_ref, at_ref[1] >= chips // 2)):

        @pl.when(inside)
        def _():
            out_ref[...] = tn(mixed_ref[0], both[...]).astype(BF16)


def grad_out_part(at, mixed_lo, mixed_hi, own, came):
    n, _, dim = mixed_lo.shape
    block, width = own.shape
    chips = n // 2
    rows = pl.BlockSpec((1, 2 * block, dim), lambda i, a: (2 * i + a[0], lax.rem(a[1], chips // 2), 0))
    return call(
        partial(grad_out_kernel, chips=chips),
        (chips,),
        [rows, rows, resident(own), resident(came)],
        pl.BlockSpec((dim, width), lambda i, a: (i, 0)),
        bf16(chips * dim, width),
        "grad_out_part",
        4 * block * chips * dim * width,
        2 * chips * dim * (4 * block + width),
        scratch=[pltpu.VMEM((2 * block, width), BF16)],
        vmem=40,
    )(at, mixed_lo, mixed_hi, own, came)


def input_grad_kernel(at_ref, kept_ref, came_ref, grad_ref, x_ref, out_ref):
    total = kept_ref[...].astype(F32) + came_ref[...].astype(F32)
    out_ref[...] = grad_ref[...] + norm_back(*normalize(x_ref[...].astype(F32)), total)


def input_grad_rows(at, kept, came, grad, x, part=64):
    block, width = grad.shape
    part = min(part, block)
    count = block // part
    rows = pl.BlockSpec((part, width), lambda i, a: (i, 0))
    return call(
        input_grad_kernel,
        (count,),
        [rows, rows, rows, pl.BlockSpec((part, width), lambda i, a: ((2 * a[1] + a[0]) * count + i, 0))],
        rows,
        jax.ShapeDtypeStruct((block, width), F32),
        "input_grad",
        20 * block * width,
        14 * block * width,
        vmem=60,
    )(at, kept, came, grad, x)


def wgrad_kernel(at_ref, *refs, groups):
    out = refs[-1]
    used, col = 0, 0
    for pieces, count in groups:
        a = refs[used : used + pieces]
        used += pieces
        for _ in range(count):
            b = refs[used : used + pieces]
            used += pieces
            total = tn(a[0][...], b[0][...])
            for s in range(1, pieces):
                total = total + tn(a[s][...], b[s][...])
            out[:, col : col + total.shape[1]] = total.astype(BF16)
            col += total.shape[1]


def wgrad(at, groups, block=512):
    in_specs, args, kinds, cols, flops = [], [], [], 0, 0
    for a, bs in groups:
        for piece in a:
            array, rows, at_row = piece if isinstance(piece, tuple) else (piece, piece.shape[0], 0)
            wide = array.shape[1]
            size = min(block, wide)
            in_specs.append(pl.BlockSpec((rows, size), lambda i, g, r=at_row: (r, i)))
            args.append(array)
        for b in bs:
            for piece in b:
                array, rows, at_row = piece if isinstance(piece, tuple) else (piece, piece.shape[0], 0)
                in_specs.append(
                    pl.BlockSpec(
                        (rows, array.shape[1]), lambda i, g, r=at_row: (r, 0), pipeline_mode=pl.Buffered(1)
                    )
                )
                args.append(array)
                flops += 2 * wide * rows * array.shape[1]
            cols += array.shape[1]
        kinds.append((len(a), len(bs)))
    return call(
        partial(wgrad_kernel, groups=kinds),
        (wide // size,),
        in_specs,
        pl.BlockSpec((size, cols), lambda i, g: (i, 0)),
        bf16(wide, cols),
        "wgrad",
        flops,
        4 * wide * cols + sum(2 * x.size for x in args),
    )(at, *args)


def halve_kernel(bit_ref, a_ref, b_ref, keep_ref, send_ref):
    total = (a_ref[...].astype(F32) + b_ref[...].astype(F32)).astype(BF16)
    ours = lax.rem(pl.program_id(0), 2) == bit_ref[0]

    @pl.when(ours)
    def _():
        keep_ref[...] = total

    @pl.when(jnp.logical_not(ours))
    def _():
        send_ref[...] = total


def halve(bit, a, b):
    count, rows, width = a.shape
    one = pl.BlockSpec((1, rows, width), lambda i, s: (i, 0, 0))
    pair = pl.BlockSpec((1, rows, width), lambda i, s: (i // 2, 0, 0))
    return call(
        halve_kernel,
        (count,),
        [one, one],
        [pair, pair],
        [bf16(count // 2, rows, width)] * 2,
        "halve",
        count * rows * width,
        6 * count * rows * width,
        vmem=40,
    )(bit, a, b)


def add_kernel(at_ref, a_ref, b_ref, out_ref):
    out_ref[...] = (a_ref[...].astype(F32) + b_ref[...].astype(F32)).astype(BF16)


def add_rows(at, a, b, block=256):
    rows, width = a.shape
    one = pl.BlockSpec((block, width), lambda i, s: (i, 0))
    return call(
        add_kernel,
        (rows // block,),
        [one, one],
        one,
        bf16(rows, width),
        "add_rows",
        rows * width,
        6 * rows * width,
        vmem=40,
    )(at, a, b)


def local(layer_input, prefix_len, w_query, w_key, w_value, w_out, w_gate, w_up, w_down, cotangent):
    seq, width = layer_input.shape
    n = lax.axis_size("tensor")
    chips = n // 2
    stages = chips.bit_length() - 1
    place = lax.axis_index("tensor")
    chip, core = place // 2, lax.rem(place, 2)
    half = seq // 2
    block = seq // n
    found = [doubling_order(chips).index(z) for z in range(chips)]
    at = jnp.concatenate([jnp.stack([core, chip]), jnp.array(found)[lax.bitwise_xor(chip, jnp.arange(chips))]])
    at = at.astype(jnp.int32)
    latest = [None]

    def done(value):
        latest[0] = value
        return value

    def later(value):
        if latest[0] is None:
            return value
        return lax.optimization_barrier((value, latest[0]))[0]

    def start(x, pairs):
        return lax.ppermute(later(x), "tensor", pairs)

    swap_cores = [(t, t ^ 1) for t in range(n)]

    def chips_apart(hop):
        return [(t, t ^ (2 * hop)) for t in range(n)]

    class Scatter:
        def __init__(self, keep, sent, blocks, hop=1):
            self.held = keep.reshape(blocks, -1, keep.shape[-1])
            self.hop = hop
            if sent is None:
                self.split()
            else:
                self.coming = start(sent, swap_cores).reshape(self.held.shape)

        def split(self):
            bit = lax.rem(chip // self.hop, 2)
            pairs = self.held.reshape(self.held.shape[0] // 2, 2, -1, self.held.shape[-1])
            self.held = lax.dynamic_index_in_dim(pairs, bit, 1, False)
            self.sent = done(lax.dynamic_index_in_dim(pairs, 1 - bit, 1, False))

        def add(self):
            bit = lax.rem(chip // self.hop, 2).astype(jnp.int32)[None]
            self.held, self.sent = halve(bit, self.held, later(self.coming))
            done(self.sent)

        def send(self):
            self.coming = start(self.sent, chips_apart(self.hop))
            self.hop *= 2

        def step(self):
            self.add()
            self.send()

        def last(self):
            return self.held[0], later(self.coming)[0]

        def total(self):
            held, came = self.last()
            return held.astype(F32) + came.astype(F32)

    def half_sum(name, key):
        s = halves[name][key]
        halves[name]["sum"] = done(add_rows(at, s.held[0], later(s.coming)[0]))

    def across():
        upper = chip >= chips // 2
        sums = [later(halves[h]["sum"]) for h in ("lo", "hi")]
        kept = jnp.where(upper, sums[1], sums[0])
        sent = done(jnp.where(upper, sums[0], sums[1]))
        return kept, lax.ppermute(sent, "tensor", chips_apart(chips // 2))

    starts = {"hi": half, "lo": 0}
    hi, lo = {}, {}
    halves = {"hi": hi, "lo": lo}

    def attention(name):
        c = halves[name]
        c["mixed"], c["lse"] = attn_fwd(later(q), k, vt, prefix_len, starts[name], half)
        done(c["mixed"])

    def spread(name):
        c = halves[name]
        c["all_mixed"] = lax.all_gather(later(c["mixed"]), "tensor")

    def both_ways(name):
        c = halves[name]
        c["residual"], c["ln"], c["hidden"], c["g_gate"], c["g_up"], c["keep"], c["send"] = feed_forward(
            at, later(c["all_mixed"]), layer_input, cot, starts[name], *w_full, w_gate, w_up, w_down, block
        )
        done(c["keep"])

    part = None

    def attention_back(name):
        nonlocal part
        c = halves[name]
        first = starts[name]
        grads = attn_bwd(q, k, kt, v, c["mixed"], g_mixed, c["lse"], cos, sin, prefix_len, first, half, first, part)
        c["dq"], c["dk"], c["dv"] = grads[:3]
        part = grads[3:]
        done(c["dq"])
        c["keep"], c["send"] = sum_nt(at, [c["dq"], c["dk"], c["dv"]], [w_query, w_key, w_value], block)
        done(c["keep"])

    def to_dp(grad, dim):
        return lax.psum_scatter(grad, "dp", scatter_dimension=dim, tiled=True)

    own = chips // 2

    def rest(transfer):
        for _ in range(stages - 2):
            transfer.step()

    n_dp = lax.axis_size("dp")
    dp_place = lax.axis_index("dp")
    piece = lax.dynamic_slice_in_dim(w_out, dp_place * (width // n_dp), width // n_dp, 1)
    hop = chips // 2
    coming = start(piece, chips_apart(hop))
    cot = lax.all_gather(cotangent, "tensor", axis=0, tiled=True)
    cos, sin = rope_tables(seq)
    done(cos)
    piece = jnp.concatenate([piece, later(coming)], 0)
    first = True
    while hop > 1:
        hop //= 2
        coming = start(done(piece), chips_apart(hop))
        if first:
            ln_one, q, k, kt, v, vt = qkv(layer_input, w_query, w_key, w_value, later(cos), sin)
            done(q)
            attention("hi")
            first = False
        piece = jnp.concatenate([piece, later(coming)], 0)
    pieces = [done(piece)] + [lax.ppermute(piece, "dp", [(d, d ^ s) for d in range(n_dp)]) for s in range(1, n_dp)]
    spread("hi")
    attention("lo")
    w_mine = done(columns(dp_place.astype(jnp.int32)[None], [later(p) for p in pieces]))
    w_full = [w_mine, lax.ppermute(w_mine, "tensor", swap_cores)]
    spread("lo")
    cot = done(later(cot))
    both_ways("hi")
    hi["g_norm"] = Scatter(hi["keep"], hi["send"], own)
    hi["g_norm"].step()
    both_ways("lo")
    rest(hi["g_norm"])
    half_sum("hi", "g_norm")
    lo["g_norm"] = Scatter(lo["keep"], lo["send"], own)
    lo["g_norm"].step()
    grad_gate_up = done(
        wgrad(at, [([hi["ln"], later(lo["ln"])], [[hi["g_gate"], lo["g_gate"]], [hi["g_up"], lo["g_up"]]])])
    )
    rest(lo["g_norm"])
    half_sum("lo", "g_norm")
    grad_gate_up = to_dp(later(grad_gate_up), 0)
    kept, came = across()
    grad_down = done(wgrad(at, [([hi["hidden"], later(lo["hidden"])], [[(cot, half, 1), (cot, half, 0)]])]))
    keep, sent = ffn_out(at, later(lo["hidden"]), hi["hidden"], lo["residual"], hi["residual"], w_down)
    done(keep)
    came = done(later(came))
    grad_down = to_dp(later(grad_down), 1)
    ffn = Scatter(keep, sent, chips)
    g_res, g_res_low, by_head = block_grad(
        at, kept, later(came), lo["residual"], hi["residual"], cotangent, *w_full, n
    )
    g_mixed = lax.all_to_all(done(by_head), "tensor", 0, 0, tiled=True).reshape(seq, -1)
    g_came = start(g_res_low, swap_cores)
    ffn.add()
    g_came = done(later(g_came))
    ffn.send()
    grad_out = done(grad_out_part(at, lo["all_mixed"], hi["all_mixed"], g_res_low, later(g_came)))
    g_mixed = done(later(g_mixed))
    attention_back("hi")
    g_mixed = later(g_mixed)
    attention_back("lo")
    ffn.add()
    grad_out = to_dp(later(grad_out), 1)
    ffn.send()
    hi["g_one"] = Scatter(hi["keep"], hi["send"], own)
    lo["g_one"] = Scatter(lo["keep"], lo["send"], own)
    hi["g_one"].step()
    lo["g_one"].step()
    rows = ln_one.shape[0] // 2
    grads = done(
        wgrad(
            at, [([(later(ln_one), rows, 0), (ln_one, rows, 1)], [[lo[key], hi[key]] for key in ("dq", "dk", "dv")])]
        )
    )
    rest(hi["g_one"])
    half_sum("hi", "g_one")
    grad_gate_up = done(later(grad_gate_up).astype(F32))
    rest(ffn)
    layer_output = done(ffn.total())
    rest(lo["g_one"])
    half_sum("lo", "g_one")
    grads = to_dp(later(grads), 0)
    kept, came = across()
    grad_down = done(later(grad_down).astype(F32))
    out_sum = Scatter(later(grad_out), None, chips)
    out_sum.send()
    for _ in range(stages - 1):
        out_sum.step()
    grads = done(later(grads).astype(F32))
    input_grad = done(input_grad_rows(at, kept, later(came), g_res, layer_input))
    grad_out = done(out_sum.total())
    hid, dim = w_gate.shape[1], w_query.shape[1]
    return (
        layer_output,
        input_grad,
        grads[:, :dim],
        grads[:, dim : 2 * dim],
        grads[:, 2 * dim :],
        grad_out,
        grad_gate_up[:, :hid],
        grad_gate_up[:, hid:],
        grad_down,
    )


def solution(mesh):
    in_specs = (
        P("dp", None),
        P("dp"),
        P(None, "tensor"),
        P(None, "tensor"),
        P(None, "tensor"),
        P("tensor", None),
        P(None, "tensor"),
        P(None, "tensor"),
        P("tensor", None),
        P(("dp", "tensor"), None),
    )
    out_specs = (
        P(("dp", "tensor"), None),
        P(("dp", "tensor"), None),
        P("dp", "tensor"),
        P("dp", "tensor"),
        P("dp", "tensor"),
        P("tensor", "dp"),
        P("dp", "tensor"),
        P("dp", "tensor"),
        P("tensor", "dp"),
    )
    return jax.shard_map(local, mesh=mesh, in_specs=in_specs, out_specs=out_specs, check_vma=False)
```

```python
import math
from functools import partial

import jax
import jax.numpy as jnp
from jax import lax
from jax.experimental import pallas as pl
from jax.experimental.pallas import tpu as pltpu
from jax.sharding import PartitionSpec as P

HD = 128
EPS = 1e-05
ROPE_BASE = 10000.0
NEG = -1e30
LOG2E = math.log2(math.e)
Q_SCALE = LOG2E * HD**-0.5
F32 = jnp.float32
BF16 = jnp.bfloat16


def nt(a, b):
    return lax.dot_general(a, b, (((1,), (1,)), ((), ())), preferred_element_type=F32)


def nn(a, b):
    return lax.dot_general(a, b, (((1,), (0,)), ((), ())), preferred_element_type=F32)


def tn(a, b):
    return lax.dot_general(a, b, (((0,), (0,)), ((), ())), preferred_element_type=F32)


def normalize(values):
    centered = values - jnp.mean(values, -1, keepdims=True)
    inv_std = lax.rsqrt(jnp.mean(centered * centered, -1, keepdims=True) + EPS)
    return centered * inv_std, inv_std


def norm_back(normed, inv_std, upstream):
    first_mean = jnp.mean(upstream, -1, keepdims=True)
    second_mean = jnp.mean(upstream * normed, -1, keepdims=True)
    return inv_std * (upstream - first_mean - normed * second_mean)


def rope_tables(seq_len, coarse=64):
    inv_freq = ROPE_BASE ** (-(2.0 * jnp.arange(HD // 2, dtype=F32)) / HD)
    fine = jnp.arange(coarse, dtype=F32)[:, None] * inv_freq[None, :]
    steps = (coarse * jnp.arange(seq_len // coarse, dtype=F32))[:, None] * inv_freq[None, :]
    both = lax.optimization_barrier((jnp.cos(fine), jnp.sin(fine), jnp.cos(steps), jnp.sin(steps)))
    cb, sb, ca, sa = both[0][None], both[1][None], both[2][:, None], both[3][:, None]
    cos = (ca * cb - sa * sb).reshape(seq_len, HD // 2)
    sin = (sa * cb + ca * sb).reshape(seq_len, HD // 2)
    return jnp.concatenate([cos, cos], -1), jnp.concatenate([-sin, sin], -1)


def qkv_kernel(x_ref, wq_ref, wk_ref, wv_ref, cos_ref, sin_ref, ln_ref, q_ref, k_ref, kt_ref, v_ref, vt_ref):
    normed, _ = normalize(x_ref[...].astype(F32))
    ln = normed.astype(BF16)
    ln_ref[...] = ln
    cos, sin = cos_ref[...], sin_ref[...]
    q, k, v = nn(ln, wq_ref[...]), nn(ln, wk_ref[...]), nn(ln, wv_ref[...]).astype(BF16)
    for h in range(q.shape[1] // HD):
        at = slice(h * HD, (h + 1) * HD)
        qh, kh = q[:, at], k[:, at]
        qr = (qh * cos + pltpu.roll(qh, HD // 2, 1) * sin) * Q_SCALE
        kr = (kh * cos + pltpu.roll(kh, HD // 2, 1) * sin).astype(BF16)
        q_ref[:, at] = qr.astype(BF16)
        k_ref[:, at] = kr
        kt_ref[at, :] = kr.T
        vt_ref[at, :] = v[:, at].T
    v_ref[...] = v


def qkv(x, w_query, w_key, w_value, cos, sin, block=256):
    rows, width = x.shape
    dim = w_query.shape[1]
    by_row = lambda n: pl.BlockSpec((block, n), lambda i: (i, 0))
    whole = pl.BlockSpec((width, dim), lambda i: (0, 0))
    flipped = pl.BlockSpec((dim, block), lambda i: (0, i))
    shape = lambda *dims: jax.ShapeDtypeStruct(dims, BF16)
    return pl.pallas_call(
        qkv_kernel,
        grid=(rows // block,),
        in_specs=[by_row(width), whole, whole, whole, by_row(HD), by_row(HD)],
        out_specs=[by_row(width), by_row(dim), by_row(dim), flipped, by_row(dim), flipped],
        out_shape=[
            shape(rows, width),
            shape(rows, dim),
            shape(rows, dim),
            shape(dim, rows),
            shape(rows, dim),
            shape(dim, rows),
        ],
        compiler_params=pltpu.CompilerParams(vmem_limit_bytes=40 << 20),
        cost_estimate=pl.CostEstimate(
            flops=6 * rows * width * dim, bytes_accessed=4 * rows * width + 6 * width * dim + 10 * rows * dim, transcendentals=0
        ),
        name="qkv",
    )(x, w_query, w_key, w_value, cos, sin)


def allowed_mask(key0, q0, shape, prefix):
    cols = key0 + lax.broadcasted_iota(jnp.int32, shape, 0)
    rows = q0 + lax.broadcasted_iota(jnp.int32, shape, 1)
    return (cols <= rows) | (cols < prefix)


def key_blocks(q0, bq, bk, prefix):
    full = jnp.maximum((q0 + 1) // bk, prefix // bk)
    total = jnp.maximum((q0 + bq + bk - 1) // bk, (prefix + bk - 1) // bk)
    return full, total


def fwd_kernel(prefix_ref, q_ref, k_ref, vt_ref, o_ref, lse_ref, m_s, l_s, acc_s, *, row0, bq, bk):
    prefix = prefix_ref[0]
    q0 = row0 + pl.program_id(1) * bq
    q = q_ref[...]
    m_s[...] = jnp.full(m_s.shape, NEG, F32)
    l_s[...] = jnp.zeros(l_s.shape, F32)
    acc_s[...] = jnp.zeros(acc_s.shape, F32)

    def step(j, masked):
        k0 = pl.multiple_of(j * bk, bk)
        s = nt(k_ref[pl.ds(k0, bk), :], q)
        if masked:
            s = jnp.where(allowed_mask(k0, q0, s.shape, prefix), s, NEG)
        m_old = m_s[...]
        m_new = jnp.maximum(m_old, jnp.max(s, 0, keepdims=True))
        p = jnp.exp2(s - m_new)
        a = jnp.exp2(m_old - m_new)
        l_s[...] = l_s[...] * a + jnp.sum(p, 0, keepdims=True)
        acc_s[...] = acc_s[...] * a + nn(vt_ref[:, pl.ds(k0, bk)], p.astype(BF16))
        m_s[...] = m_new

    full, total = key_blocks(q0, bq, bk, prefix)
    lax.fori_loop(0, full, lambda j, c: (step(j, False), c)[1], 0)
    lax.fori_loop(full, total, lambda j, c: (step(j, True), c)[1], 0)
    l = l_s[...]
    o_ref[...] = (acc_s[...] / l).T.astype(BF16)
    lse_ref[...] = (m_s[...] + jnp.log2(l))[None]


def attn_fwd(q, k, vt, prefix, row0, rows, bq=512, bk=512):
    seq, dim = k.shape
    heads = dim // HD
    bq, bk = min(bq, rows), min(bk, rows)
    first = row0 // bq
    return pl.pallas_call(
        partial(fwd_kernel, row0=row0, bq=bq, bk=bk),
        grid_spec=pltpu.PrefetchScalarGridSpec(
            num_scalar_prefetch=1,
            grid=(heads, rows // bq),
            in_specs=[
                pl.BlockSpec((bq, HD), lambda h, i, p: (i + first, h)),
                pl.BlockSpec((seq, HD), lambda h, i, p: (0, h)),
                pl.BlockSpec((HD, seq), lambda h, i, p: (h, 0)),
            ],
            out_specs=[
                pl.BlockSpec((bq, HD), lambda h, i, p: (i, h)),
                pl.BlockSpec((1, 1, bq), lambda h, i, p: (h, 0, i)),
            ],
            scratch_shapes=[
                pltpu.VMEM((1, bq), F32),
                pltpu.VMEM((1, bq), F32),
                pltpu.VMEM((HD, bq), F32),
            ],
        ),
        out_shape=[
            jax.ShapeDtypeStruct((rows, dim), BF16),
            jax.ShapeDtypeStruct((heads, 1, rows), F32),
        ],
        compiler_params=pltpu.CompilerParams(vmem_limit_bytes=32 << 20),
        cost_estimate=pl.CostEstimate(
            flops=12 * rows * seq * dim, bytes_accessed=4 * seq * dim + 4 * rows * dim, transcendentals=rows * seq * heads
        ),
        name="attn_fwd",
    )(prefix, q, k, vt)


def unrope(t, cos, sin):
    return t * cos - pltpu.roll(t, HD // 2, 1) * sin


def bwd_kernel(prefix_ref, q_ref, k_ref, kt_ref, v_ref, o_ref, do_ref, lse_ref, cq_ref, sq_ref, ck_ref, sk_ref, *rest, row0, bq, bk, keys, has_in, lo):
    rest = list(rest)
    if has_in:
        dk_in, dv_in = rest[:2]
        rest = rest[2:]
    dq_ref, dk_ref, dv_ref = rest[:3]
    rest = rest[3:]
    if lo:
        dk_part, dv_part = rest[:2]
        rest = rest[2:]
    dk_s, dv_s, dq_s = rest
    qi = pl.program_id(1)
    prefix = prefix_ref[0]
    q0 = row0 + qi * bq

    @pl.when(qi == 0)
    def _():
        if has_in:
            dk_s[...] = dk_in[...]
            dv_s[...] = dv_in[...]
        else:
            dk_s[...] = jnp.zeros(dk_s.shape, F32)
            dv_s[...] = jnp.zeros(dv_s.shape, F32)

    q, do = q_ref[...], do_ref[...]
    lse = lse_ref[0]
    delta = jnp.sum((do.astype(F32) * o_ref[...].astype(F32)).T, 0, keepdims=True)
    dq_s[...] = jnp.zeros(dq_s.shape, F32)

    def step(j, masked):
        k0 = pl.multiple_of(j * bk, bk)
        at = pl.ds(k0, bk)
        s = nt(k_ref[at, :], q)
        p = jnp.exp2(s - lse)
        if masked:
            p = jnp.where(allowed_mask(k0, q0, s.shape, prefix), p, 0.0)
        dp = nt(v_ref[at, :], do)
        ds = (p * (dp - delta)).astype(BF16)
        dv_s[at, :] += nn(p.astype(BF16), do)
        dk_s[at, :] += nn(ds, q)
        dq_s[...] += nn(kt_ref[:, at], ds)

    full, total = key_blocks(q0, bq, bk, prefix)
    lax.fori_loop(0, full, lambda j, c: (step(j, False), c)[1], 0)
    lax.fori_loop(full, total, lambda j, c: (step(j, True), c)[1], 0)
    dq_ref[...] = unrope((dq_s[...] * HD**-0.5).T, cq_ref[...], sq_ref[...]).astype(BF16)

    @pl.when(qi == pl.num_programs(1) - 1)
    def _():
        dk_ref[...] = unrope(dk_s[lo:keys, :] * (1.0 / LOG2E), ck_ref[...], sk_ref[...]).astype(BF16)
        dv_ref[...] = dv_s[lo:keys, :].astype(BF16)
        if lo:
            dk_part[...] = dk_s[:lo, :]
            dv_part[...] = dv_s[:lo, :]


def attn_bwd(q, k, kt, v, o, do, lse, cos, sin, prefix, row0, rows, lo, part=None, bq=512, bk=512):
    dim = k.shape[1]
    heads = dim // HD
    keys = row0 + rows
    own = keys - lo
    bq, bk = min(bq, rows), min(bk, rows)
    first = row0 // bq
    has_in = part is not None
    full = lambda n: pl.BlockSpec((n, HD), lambda h, i, p: (0, h))
    table_q = pl.BlockSpec((bq, HD), lambda h, i, p: (i + first, 0))
    table_k = pl.BlockSpec((own, HD), lambda h, i, p: (lo // own, 0))
    by_q = pl.BlockSpec((bq, HD), lambda h, i, p: (i, h))
    in_specs = [
        pl.BlockSpec((bq, HD), lambda h, i, p: (i + first, h)),
        full(keys),
        pl.BlockSpec((HD, keys), lambda h, i, p: (h, 0)),
        full(keys),
        by_q,
        pl.BlockSpec((bq, HD), lambda h, i, p: (i + first, h)),
        pl.BlockSpec((1, 1, bq), lambda h, i, p: (h, 0, i)),
        table_q,
        table_q,
        table_k,
        table_k,
    ]
    args = [q, k, kt, v, o, do, lse, cos, sin, cos, sin]
    if has_in:
        in_specs += [full(keys), full(keys)]
        args += list(part)
    out_specs = [by_q, full(own), full(own)]
    out_shape = [jax.ShapeDtypeStruct((rows, dim), BF16)] + [jax.ShapeDtypeStruct((own, dim), BF16)] * 2
    if lo:
        out_specs += [full(lo), full(lo)]
        out_shape += [jax.ShapeDtypeStruct((lo, dim), F32)] * 2
    return pl.pallas_call(
        partial(bwd_kernel, row0=row0, bq=bq, bk=bk, keys=keys, has_in=has_in, lo=lo),
        grid_spec=pltpu.PrefetchScalarGridSpec(
            num_scalar_prefetch=1,
            grid=(heads, rows // bq),
            in_specs=in_specs,
            out_specs=out_specs,
            scratch_shapes=[
                pltpu.VMEM((keys, HD), F32),
                pltpu.VMEM((keys, HD), F32),
                pltpu.VMEM((HD, bq), F32),
            ],
        ),
        out_shape=out_shape,
        compiler_params=pltpu.CompilerParams(vmem_limit_bytes=48 << 20),
        cost_estimate=pl.CostEstimate(
            flops=24 * rows * keys * dim, bytes_accessed=8 * keys * dim + 8 * rows * dim, transcendentals=rows * keys * heads
        ),
        name="attn_bwd",
    )(prefix, *args)


def resident(a):
    return pl.BlockSpec(a.shape, lambda *_: (0,) * a.ndim, pipeline_mode=pl.Buffered(1))


def call(kernel, grid, in_specs, out_specs, out_shape, name, flops, traffic, scratch=(), prefetch=1, vmem=56, exps=0):
    return pl.pallas_call(
        kernel,
        grid_spec=pltpu.PrefetchScalarGridSpec(
            num_scalar_prefetch=prefetch,
            grid=grid,
            in_specs=in_specs,
            out_specs=out_specs,
            scratch_shapes=list(scratch),
        ),
        out_shape=out_shape,
        compiler_params=pltpu.CompilerParams(vmem_limit_bytes=vmem << 20),
        cost_estimate=pl.CostEstimate(flops=flops, bytes_accessed=traffic, transcendentals=exps),
        name=name,
    )


def bf16(*dims):
    return jax.ShapeDtypeStruct(dims, BF16)


def by_core(at_ref, keep_ref, send_ref, value):
    ours = lax.rem(pl.program_id(0), 2) == at_ref[0]

    @pl.when(ours)
    def _():
        keep_ref[...] = value

    @pl.when(jnp.logical_not(ours))
    def _():
        send_ref[...] = value


def half_blocks(block, width):
    return [pl.BlockSpec((block, width), lambda i, a: (i // 2, 0))] * 2


def sum_nt_kernel(at_ref, *refs, terms):
    xs, ws, (keep_ref, send_ref) = refs[:terms], refs[terms : 2 * terms], refs[2 * terms :]
    total = nt(xs[0][...], ws[0][...])
    for x, w in zip(xs[1:], ws[1:]):
        total = total + nt(x[...], w[...])
    by_core(at_ref, keep_ref, send_ref, total.astype(BF16))


def sum_nt(at, xs, ws, block):
    rows = xs[0].shape[0]
    depth = sum(x.shape[1] for x in xs)
    width = ws[0].shape[0]
    return call(
        partial(sum_nt_kernel, terms=len(xs)),
        (rows // block,),
        [pl.BlockSpec((block, x.shape[1]), lambda i, a: (i, 0)) for x in xs] + [resident(w) for w in ws],
        half_blocks(block, width),
        [bf16(rows // 2, width)] * 2,
        "sum_nt",
        2 * rows * depth * width,
        2 * rows * (depth + width) + 2 * depth * width,
        vmem=40,
    )(at, *xs, *ws)


def doubling_order(chips):
    order, hop = [0], chips // 2
    while hop:
        order = order + [o ^ hop for o in order]
        hop //= 2
    return order


def ff_kernel(
    at_ref, mixed_ref, x_ref, cot_ref, wm_any, wo_any, wg_any, wu_any, wd_any,
    res_ref, ln_ref, hid_ref, gg_ref, gu_ref, keep_ref, send_ref,
    mine, other, wm_ref, wo_ref, wg_ref, wu_ref, wd_ref, sems, *, first,
):
    core, chip = at_ref[0], at_ref[1]
    dim = mixed_ref.shape[2]
    weights = ((wm_any, wm_ref), (wo_any, wo_ref), (wg_any, wg_ref), (wu_any, wu_ref), (wd_any, wd_ref))
    copies = [pltpu.make_async_copy(source, held, sems.at[s]) for s, (source, held) in enumerate(weights)]

    @pl.when(pl.program_id(0) == 0)
    def _():
        for copy in copies:
            copy.start()

    def need(s):
        @pl.when(pl.program_id(0) == 0)
        def _():
            copies[s].wait()

    chips = mixed_ref.shape[0] // 2
    for j, away in enumerate(doubling_order(chips)):
        z = lax.bitwise_xor(chip, away)
        cols = slice(j * dim, (j + 1) * dim)
        mine[:, cols] = mixed_ref[2 * z + core]
        other[:, cols] = mixed_ref[2 * z + 1 - core]
    need(0)
    residual = x_ref[...].astype(F32) + nn(mine[...], wm_ref[...])
    need(1)
    residual = residual + nn(other[...], wo_ref[...])

    @pl.when(pl.program_id(0) + first == 2 * chip + core)
    def _():
        res_ref[...] = residual

    normed, _ = normalize(residual)
    ln = normed.astype(BF16)
    ln_ref[...] = ln
    need(2)
    gate = nn(ln, wg_ref[...])
    need(3)
    up = nn(ln, wu_ref[...])
    need(4)
    grad = nt(cot_ref[...], wd_ref[...])
    sig = 1.0 / (1.0 + jnp.exp(-gate))
    act = gate * sig
    hid_ref[...] = (act * up).astype(BF16)
    gg = (grad * up * sig * (1.0 + gate * (1.0 - sig))).astype(BF16)
    gu = (grad * act).astype(BF16)
    gg_ref[...] = gg
    gu_ref[...] = gu
    by_core(at_ref, keep_ref, send_ref, (nt(gg, wg_ref[...]) + nt(gu, wu_ref[...])).astype(BF16))


def feed_forward(at, mixed, x, cot, row0, w_mine, w_other, w_gate, w_up, w_down, block):
    n, rows, dim = mixed.shape
    width = x.shape[1]
    hid = w_gate.shape[1]
    first = row0 // block
    by_row = lambda n, f=0: pl.BlockSpec((block, n), lambda i, a: (i + f, 0))
    return call(
        partial(ff_kernel, first=first),
        (rows // block,),
        [
            pl.BlockSpec((n, block, dim), lambda i, a: (0, i, 0)),
            by_row(width, first),
            by_row(width, first),
        ]
        + [pl.BlockSpec(memory_space=pl.ANY)] * 5,
        [pl.BlockSpec((block, width), lambda i, a: (0, 0)), by_row(width), by_row(hid), by_row(hid), by_row(hid)]
        + half_blocks(block, width),
        [jax.ShapeDtypeStruct((block, width), F32), bf16(rows, width)]
        + [bf16(rows, hid)] * 3
        + [bf16(rows // 2, width)] * 2,
        "feed_forward",
        10 * rows * width * hid + 2 * rows * width * width,
        6 * width * hid + 2 * width * width + 10 * rows * width + 6 * rows * hid,
        scratch=[pltpu.VMEM((block, n * dim // 2), BF16)] * 2
        + [pltpu.VMEM(w.shape, BF16) for w in (w_mine, w_other, w_gate, w_up, w_down)]
        + [pltpu.SemaphoreType.DMA((5,))],
        exps=rows * hid,
    )(at, mixed, x, cot, w_mine, w_other, w_gate, w_up, w_down)


def ffn_out_kernel(at_ref, lo_ref, hi_ref, rlo_ref, rhi_ref, w_ref, keep_ref, send_ref, out, *, steps):
    step = pl.program_id(0)
    ours = step == 2 * at_ref[1] + at_ref[0]
    for hid_ref, res_ref, inside in ((lo_ref, rlo_ref, step < steps // 2), (hi_ref, rhi_ref, step >= steps // 2)):

        @pl.when(inside)
        def _():
            out[...] = nn(hid_ref[...], w_ref[...])

        @pl.when(jnp.logical_and(inside, ours))
        def _():
            out[...] = out[...] + res_ref[...]

    by_core(at_ref, keep_ref, send_ref, out[...].astype(BF16))


def ffn_out(at, hid_lo, hid_hi, res_lo, res_hi, w_down):
    half, hid = hid_lo.shape
    block, width = res_lo.shape
    steps = 2 * half // block
    per = steps // 2
    return call(
        partial(ffn_out_kernel, steps=steps),
        (steps,),
        [
            pl.BlockSpec((block, hid), lambda i, a: (jnp.minimum(i, per - 1), 0)),
            pl.BlockSpec((block, hid), lambda i, a: (jnp.maximum(i - per, 0), 0)),
            resident(res_lo),
            resident(res_hi),
            resident(w_down),
        ],
        half_blocks(block, width),
        [bf16(half, width)] * 2,
        "ffn_out",
        4 * half * hid * width,
        4 * half * (hid + width) + 2 * hid * width,
        scratch=[pltpu.VMEM((block, width), F32)],
        vmem=40,
    )(at, hid_lo, hid_hi, res_lo, res_hi, w_down)


def columns_kernel(dp_ref, *refs):
    pieces, out = refs[:-1], refs[-1]
    for s, piece in enumerate(pieces):

        @pl.when(lax.bitwise_xor(dp_ref[0], pl.program_id(0)) == s)
        def _():
            out[...] = piece[...]


def columns(dp, pieces):
    rows, part = pieces[0].shape
    n = len(pieces)
    return call(
        columns_kernel,
        (n,),
        [resident(p) for p in pieces],
        pl.BlockSpec((rows, part), lambda i, a: (0, i)),
        bf16(rows, n * part),
        "columns",
        0,
        4 * n * rows * part,
        vmem=40,
    )(dp, *pieces)


def block_grad_kernel(at_ref, held_ref, came_ref, rlo_ref, rhi_ref, cot_ref, wm_ref, wo_ref, grad_ref, low_ref, out_ref, *, chips):
    for res_ref, inside in ((rlo_ref, at_ref[1] < chips // 2), (rhi_ref, at_ref[1] >= chips // 2)):

        @pl.when(jnp.logical_and(pl.program_id(0) == 0, inside))
        def _():
            total = held_ref[...].astype(F32) + came_ref[...].astype(F32)
            grad = cot_ref[...].astype(F32) + norm_back(*normalize(res_ref[...]), total)
            grad_ref[...] = grad
            low_ref[...] = grad.astype(BF16)

    ours = lax.rem(pl.program_id(0), 2) == at_ref[0]

    @pl.when(ours)
    def _():
        out_ref[0] = nt(low_ref[...], wm_ref[...]).astype(BF16)

    @pl.when(jnp.logical_not(ours))
    def _():
        out_ref[0] = nt(low_ref[...], wo_ref[...]).astype(BF16)


def block_grad(at, held, came, res_lo, res_hi, cotangent, w_mine, w_other, n):
    block, width = cotangent.shape
    dim = w_mine.shape[0] * 2 // n
    one = pl.BlockSpec((block, width), lambda i, a: (0, 0))
    by_chip = pl.BlockSpec((dim, width), lambda i, a: (a[2 + i // 2], 0))
    return call(
        partial(block_grad_kernel, chips=n // 2),
        (n,),
        [one, one, one, one, one, by_chip, by_chip],
        [one, one, pl.BlockSpec((1, block, dim), lambda i, a: (i, 0, 0))],
        [jax.ShapeDtypeStruct((block, width), F32), bf16(block, width), bf16(n, block, dim)],
        "block_grad",
        2 * block * width * width,
        2 * width * width + 20 * block * width,
    )(at, held, came, res_lo, res_hi, cotangent, w_mine, w_other)


def grad_out_kernel(at_ref, mlo_ref, mhi_ref, own_ref, came_ref, out_ref, both, *, chips):
    block = own_ref.shape[0]
    core = at_ref[0]

    @pl.when(pl.program_id(0) == 0)
    def _():
        both[pl.ds(pl.multiple_of(core * block, block), block), :] = own_ref[...]
        both[pl.ds(pl.multiple_of((1 - core) * block, block), block), :] = came_ref[...]

    for mixed_ref, inside in ((mlo_ref, at_ref[1] < chips // 2), (mhi_ref, at_ref[1] >= chips // 2)):

        @pl.when(inside)
        def _():
            out_ref[...] = tn(mixed_ref[0], both[...]).astype(BF16)


def grad_out_part(at, mixed_lo, mixed_hi, own, came):
    n, _, dim = mixed_lo.shape
    block, width = own.shape
    chips = n // 2
    rows = pl.BlockSpec((1, 2 * block, dim), lambda i, a: (2 * i + a[0], lax.rem(a[1], chips // 2), 0))
    return call(
        partial(grad_out_kernel, chips=chips),
        (chips,),
        [rows, rows, resident(own), resident(came)],
        pl.BlockSpec((dim, width), lambda i, a: (i, 0)),
        bf16(chips * dim, width),
        "grad_out_part",
        4 * block * chips * dim * width,
        2 * chips * dim * (4 * block + width),
        scratch=[pltpu.VMEM((2 * block, width), BF16)],
        vmem=40,
    )(at, mixed_lo, mixed_hi, own, came)


def input_grad_kernel(at_ref, kept_ref, came_ref, grad_ref, x_ref, out_ref):
    total = kept_ref[...].astype(F32) + came_ref[...].astype(F32)
    out_ref[...] = grad_ref[...] + norm_back(*normalize(x_ref[...].astype(F32)), total)


def input_grad_rows(at, kept, came, grad, x, part=64):
    block, width = grad.shape
    part = min(part, block)
    count = block // part
    rows = pl.BlockSpec((part, width), lambda i, a: (i, 0))
    return call(
        input_grad_kernel,
        (count,),
        [rows, rows, rows, pl.BlockSpec((part, width), lambda i, a: ((2 * a[1] + a[0]) * count + i, 0))],
        rows,
        jax.ShapeDtypeStruct((block, width), F32),
        "input_grad",
        20 * block * width,
        14 * block * width,
        vmem=60,
    )(at, kept, came, grad, x)


def wgrad_kernel(at_ref, *refs, groups):
    out = refs[-1]
    used, col = 0, 0
    for pieces, count in groups:
        a = refs[used : used + pieces]
        used += pieces
        for _ in range(count):
            b = refs[used : used + pieces]
            used += pieces
            total = tn(a[0][...], b[0][...])
            for s in range(1, pieces):
                total = total + tn(a[s][...], b[s][...])
            out[:, col : col + total.shape[1]] = total.astype(BF16)
            col += total.shape[1]


def wgrad(at, groups, block=512):
    in_specs, args, kinds, cols, flops = [], [], [], 0, 0
    for a, bs in groups:
        for piece in a:
            array, rows, at_row = piece if isinstance(piece, tuple) else (piece, piece.shape[0], 0)
            wide = array.shape[1]
            size = min(block, wide)
            in_specs.append(pl.BlockSpec((rows, size), lambda i, g, r=at_row: (r, i)))
            args.append(array)
        for b in bs:
            for piece in b:
                array, rows, at_row = piece if isinstance(piece, tuple) else (piece, piece.shape[0], 0)
                in_specs.append(
                    pl.BlockSpec(
                        (rows, array.shape[1]), lambda i, g, r=at_row: (r, 0), pipeline_mode=pl.Buffered(1)
                    )
                )
                args.append(array)
                flops += 2 * wide * rows * array.shape[1]
            cols += array.shape[1]
        kinds.append((len(a), len(bs)))
    return call(
        partial(wgrad_kernel, groups=kinds),
        (wide // size,),
        in_specs,
        pl.BlockSpec((size, cols), lambda i, g: (i, 0)),
        bf16(wide, cols),
        "wgrad",
        flops,
        4 * wide * cols + sum(2 * x.size for x in args),
    )(at, *args)


def halve_kernel(bit_ref, a_ref, b_ref, keep_ref, send_ref):
    total = (a_ref[...].astype(F32) + b_ref[...].astype(F32)).astype(BF16)
    ours = lax.rem(pl.program_id(0), 2) == bit_ref[0]

    @pl.when(ours)
    def _():
        keep_ref[...] = total

    @pl.when(jnp.logical_not(ours))
    def _():
        send_ref[...] = total


def halve(bit, a, b):
    count, rows, width = a.shape
    one = pl.BlockSpec((1, rows, width), lambda i, s: (i, 0, 0))
    pair = pl.BlockSpec((1, rows, width), lambda i, s: (i // 2, 0, 0))
    return call(
        halve_kernel,
        (count,),
        [one, one],
        [pair, pair],
        [bf16(count // 2, rows, width)] * 2,
        "halve",
        count * rows * width,
        6 * count * rows * width,
        vmem=40,
    )(bit, a, b)


def add_kernel(at_ref, a_ref, b_ref, out_ref):
    out_ref[...] = (a_ref[...].astype(F32) + b_ref[...].astype(F32)).astype(BF16)


def add_rows(at, a, b, block=256):
    rows, width = a.shape
    one = pl.BlockSpec((block, width), lambda i, s: (i, 0))
    return call(
        add_kernel,
        (rows // block,),
        [one, one],
        one,
        bf16(rows, width),
        "add_rows",
        rows * width,
        6 * rows * width,
        vmem=40,
    )(at, a, b)


def local(layer_input, prefix_len, w_query, w_key, w_value, w_out, w_gate, w_up, w_down, cotangent):
    seq, width = layer_input.shape
    n = lax.axis_size("tensor")
    chips = n // 2
    stages = chips.bit_length() - 1
    place = lax.axis_index("tensor")
    chip, core = place // 2, lax.rem(place, 2)
    half = seq // 2
    block = seq // n
    found = [doubling_order(chips).index(z) for z in range(chips)]
    at = jnp.concatenate([jnp.stack([core, chip]), jnp.array(found)[lax.bitwise_xor(chip, jnp.arange(chips))]])
    at = at.astype(jnp.int32)
    latest = [None]

    def done(value):
        latest[0] = value
        return value

    def later(value):
        if latest[0] is None:
            return value
        return lax.optimization_barrier((value, latest[0]))[0]

    def start(x, pairs):
        return lax.ppermute(later(x), "tensor", pairs)

    swap_cores = [(t, t ^ 1) for t in range(n)]

    def chips_apart(hop):
        return [(t, t ^ (2 * hop)) for t in range(n)]

    class Scatter:
        def __init__(self, keep, sent, blocks, hop=1):
            self.held = keep.reshape(blocks, -1, keep.shape[-1])
            self.hop = hop
            if sent is None:
                self.split()
            else:
                self.coming = start(sent, swap_cores).reshape(self.held.shape)

        def split(self):
            bit = lax.rem(chip // self.hop, 2)
            pairs = self.held.reshape(self.held.shape[0] // 2, 2, -1, self.held.shape[-1])
            self.held = lax.dynamic_index_in_dim(pairs, bit, 1, False)
            self.sent = done(lax.dynamic_index_in_dim(pairs, 1 - bit, 1, False))

        def add(self):
            bit = lax.rem(chip // self.hop, 2).astype(jnp.int32)[None]
            self.held, self.sent = halve(bit, self.held, later(self.coming))
            done(self.sent)

        def send(self):
            self.coming = start(self.sent, chips_apart(self.hop))
            self.hop *= 2

        def step(self):
            self.add()
            self.send()

        def last(self):
            return self.held[0], later(self.coming)[0]

        def total(self):
            held, came = self.last()
            return held.astype(F32) + came.astype(F32)

    def half_sum(name, key, fold=False):
        s = halves[name][key]
        if fold:
            came = done(later(s.coming)[0])
            halves[name]["sum"] = (s.held[0].astype(F32) + came.astype(F32)).astype(BF16)
        else:
            halves[name]["sum"] = done(add_rows(at, s.held[0], later(s.coming)[0]))

    def across():
        upper = chip >= chips // 2
        low, high = lo["sum"], later(hi["sum"])
        kept = jnp.where(upper, high, low)
        sent = done(jnp.where(upper, low, high))
        return kept, lax.ppermute(sent, "tensor", chips_apart(chips // 2))

    starts = {"hi": half, "lo": 0}
    hi, lo = {}, {}
    halves = {"hi": hi, "lo": lo}

    def attention(name):
        c = halves[name]
        c["mixed"], c["lse"] = attn_fwd(later(q), k, vt, prefix_len, starts[name], half)
        done(c["mixed"])

    def spread(name):
        c = halves[name]
        c["all_mixed"] = lax.all_gather(later(c["mixed"]), "tensor")

    def both_ways(name):
        c = halves[name]
        c["residual"], c["ln"], c["hidden"], c["g_gate"], c["g_up"], c["keep"], c["send"] = feed_forward(
            at, later(c["all_mixed"]), layer_input, cot, starts[name], *w_full, w_gate, w_up, w_down, block
        )
        done(c["keep"])

    part = None

    def attention_back(name):
        nonlocal part
        c = halves[name]
        first = starts[name]
        grads = attn_bwd(q, k, kt, v, c["mixed"], g_mixed, c["lse"], cos, sin, prefix_len, first, half, first, part)
        c["dq"], c["dk"], c["dv"] = grads[:3]
        part = grads[3:]
        done(c["dq"])
        c["keep"], c["send"] = sum_nt(at, [c["dq"], c["dk"], c["dv"]], [w_query, w_key, w_value], block)
        done(c["keep"])

    def to_dp(grad, dim):
        return lax.psum_scatter(grad, "dp", scatter_dimension=dim, tiled=True)

    own = chips // 2

    def rest(transfer):
        for _ in range(stages - 2):
            transfer.step()

    n_dp = lax.axis_size("dp")
    dp_place = lax.axis_index("dp")
    piece = lax.dynamic_slice_in_dim(w_out, dp_place * (width // n_dp), width // n_dp, 1)
    hop = chips // 2
    coming = start(piece, chips_apart(hop))
    cot = lax.all_gather(cotangent, "tensor", axis=0, tiled=True)
    cos, sin = rope_tables(seq)
    done(cos)
    piece = jnp.concatenate([piece, later(coming)], 0)
    first = True
    while hop > 1:
        hop //= 2
        coming = start(done(piece), chips_apart(hop))
        if first:
            ln_one, q, k, kt, v, vt = qkv(layer_input, w_query, w_key, w_value, later(cos), sin)
            done(q)
            attention("hi")
            first = False
        piece = jnp.concatenate([piece, later(coming)], 0)
    pieces = [done(piece)] + [lax.ppermute(piece, "dp", [(d, d ^ s) for d in range(n_dp)]) for s in range(1, n_dp)]
    spread("hi")
    attention("lo")
    w_mine = done(columns(dp_place.astype(jnp.int32)[None], [later(p) for p in pieces]))
    w_full = [w_mine, lax.ppermute(w_mine, "tensor", swap_cores)]
    spread("lo")
    cot = done(later(cot))
    both_ways("hi")
    hi["g_norm"] = Scatter(hi["keep"], hi["send"], own)
    hi["g_norm"].step()
    both_ways("lo")
    rest(hi["g_norm"])
    half_sum("hi", "g_norm")
    lo["g_norm"] = Scatter(lo["keep"], lo["send"], own)
    lo["g_norm"].step()
    grad_gate_up = done(
        wgrad(at, [([hi["ln"], later(lo["ln"])], [[hi["g_gate"], lo["g_gate"]], [hi["g_up"], lo["g_up"]]])])
    )
    rest(lo["g_norm"])
    half_sum("lo", "g_norm", True)
    grad_gate_up = to_dp(later(grad_gate_up), 0)
    kept, came = across()
    grad_down = done(wgrad(at, [([hi["hidden"], later(lo["hidden"])], [[(cot, half, 1), (cot, half, 0)]])]))
    keep, sent = ffn_out(at, later(lo["hidden"]), hi["hidden"], lo["residual"], hi["residual"], w_down)
    done(keep)
    came = done(later(came))
    grad_down = to_dp(later(grad_down), 1)
    ffn = Scatter(keep, sent, chips)
    g_res, g_res_low, by_head = block_grad(
        at, kept, later(came), lo["residual"], hi["residual"], cotangent, *w_full, n
    )
    g_mixed = lax.all_to_all(done(by_head), "tensor", 0, 0, tiled=True).reshape(seq, -1)
    g_came = start(g_res_low, swap_cores)
    ffn.add()
    g_came = done(later(g_came))
    ffn.send()
    grad_out = done(grad_out_part(at, lo["all_mixed"], hi["all_mixed"], g_res_low, later(g_came)))
    g_mixed = done(later(g_mixed))
    attention_back("hi")
    g_mixed = later(g_mixed)
    attention_back("lo")
    ffn.add()
    grad_out = to_dp(later(grad_out), 1)
    ffn.send()
    hi["g_one"] = Scatter(hi["keep"], hi["send"], own)
    lo["g_one"] = Scatter(lo["keep"], lo["send"], own)
    hi["g_one"].step()
    lo["g_one"].step()
    rows = ln_one.shape[0] // 2
    grads = done(
        wgrad(
            at, [([(later(ln_one), rows, 0), (ln_one, rows, 1)], [[lo[key], hi[key]] for key in ("dq", "dk", "dv")])]
        )
    )
    rest(hi["g_one"])
    half_sum("hi", "g_one")
    grad_gate_up = done(later(grad_gate_up).astype(F32))
    rest(ffn)
    layer_output = done(ffn.total())
    rest(lo["g_one"])
    half_sum("lo", "g_one", True)
    grads = to_dp(later(grads), 0)
    kept, came = across()
    grad_down = done(later(grad_down).astype(F32))
    out_sum = Scatter(later(grad_out), None, chips)
    out_sum.send()
    for _ in range(stages - 1):
        out_sum.step()
    grads = done(later(grads).astype(F32))
    input_grad = done(input_grad_rows(at, kept, later(came), g_res, layer_input))
    grad_out = done(out_sum.total())
    hid, dim = w_gate.shape[1], w_query.shape[1]
    return (
        layer_output,
        input_grad,
        grads[:, :dim],
        grads[:, dim : 2 * dim],
        grads[:, 2 * dim :],
        grad_out,
        grad_gate_up[:, :hid],
        grad_gate_up[:, hid:],
        grad_down,
    )


def solution(mesh):
    in_specs = (
        P("dp", None),
        P("dp"),
        P(None, "tensor"),
        P(None, "tensor"),
        P(None, "tensor"),
        P("tensor", None),
        P(None, "tensor"),
        P(None, "tensor"),
        P("tensor", None),
        P(("dp", "tensor"), None),
    )
    out_specs = (
        P(("dp", "tensor"), None),
        P(("dp", "tensor"), None),
        P("dp", "tensor"),
        P("dp", "tensor"),
        P("dp", "tensor"),
        P("tensor", "dp"),
        P("dp", "tensor"),
        P("dp", "tensor"),
        P("tensor", "dp"),
    )
    return jax.shard_map(local, mesh=mesh, in_specs=in_specs, out_specs=out_specs, check_vma=False)
```
